32 devices in a mesh: grp: 4 (over x, core), dev: 8 (over z, y).
Axes of the slice: x: 2, y: 2, z: 4, core: 2. Of those that a mesh axis runs over, the one named last changes fastest.
Arguments:
- tracer: float32 [96, 131072], P(None, ('grp', 'dev')), may hold values from 0.05 to 2
- tile_rows: int32 [5120], P(('grp', 'dev')), may hold values from 0 to 1023, as said below
- tile_cols: int32 [5120], P(('grp', 'dev')), may hold values from 0 to 1023, as said below
- tile_values: bfloat16 [5120, 128, 128], P(('grp', 'dev')), may hold values from -0.25 to 0.25
- level_counts: int32 [4096], P(('grp', 'dev')), may hold values from 1 to 32, as said below
- column_owner: int32 [4096], P(('grp', 'dev')), may hold values from 0 to 7, as said below
- half_saturation: float32 [16], replicated, may hold values from 0.1 to 1
- growth_rate: float32 [64], replicated, may hold values from 0.2 to 2
- uptake: float32 [64, 16], replicated, may hold values from 0 to 0.125
- graze_preference: float32 [64, 64], replicated, may hold values from 0 to 0.03125
- graze_maximum: float32 [64], replicated, may hold values from 0.2 to 2
Outputs:
- updated: float32 [96, 131072], P(None, ('grp', 'dev'))
- production: float32 [4096], P(('grp', 'dev'))
The draws below stay inside these ranges and needn't reach their ends.
Inputs may be any that keep to these rules, and one draw needn't show every extreme that they name: `tile_rows`: each device holds 160 tiles; taken device after device along dev, the tiles of a group run in increasing row block. Device d of the whole chain of devices owns row blocks d * 32 to d * 32 + 31; its tiles have row blocks of its own or, among its first 20 tiles only, of the device before it in its group. Device 1 of every group holds exactly 20 tiles of device 0's row blocks. `tile_cols`: A tile's column block lies within 16 blocks of its row block, and within the blocks owned by the device that holds the tile and its two neighbours in the chain. `level_counts`: every device's first column has 32 wet levels, its second one 1. `column_owner`: every device sends exactly 16 of its columns to each device of its group.
All inputs are finite; a program needn't handle non-finite values.
Results may differ from the reference program's by a relative error of at most 0.0018.
Values may be sent and summed in bfloat16 or wider, within the bound.
No kernel may reach another device: no remote copies, remote signals or barrier semaphores. Data moves between devices by JAX's collectives and lax.ppermute only.
A program may use at most 64 MiB of HBM per device.

```python
import math
import jax
import jax.numpy as jnp
from jax import lax

NUT = 16
PLK = 64
NTR = 96
LEV = 32
COLS_DEV = 128
BLK = 128
TPB = 5
CD = 4096
BPD = 32
NT = 160
SPILL = 20
R = 16
NCELL = 131072
TILES = 5120
N_GRP = 4
N_DEV = 8


def tile_pattern(key):
    device_count = N_GRP * N_DEV
    spill_key = jax.random.fold_in(key, 11)
    offset_key = jax.random.fold_in(key, 12)
    owner_ids = jnp.arange(N_DEV, dtype=jnp.int32)
    spill_count = jax.random.randint(spill_key, (N_GRP, N_DEV), 0, SPILL + 1)
    spill_count = jnp.where(owner_ids[None, :] == 0, SPILL, spill_count)
    spill_count = jnp.where(owner_ids[None, :] == N_DEV - 1, 0, spill_count)
    range_end = (owner_ids[None, :] + 1) * NT + spill_count
    range_start = jnp.concatenate([jnp.zeros((N_GRP, 1), jnp.int32), range_end[:, :-1]], axis=1)
    position = jnp.arange(N_DEV * NT, dtype=jnp.int32)
    owner_index = jnp.sum((range_end[:, None, :] <= position[None, :, None]).astype(jnp.int32), axis=2)
    first_tile = jnp.take_along_axis(range_start, owner_index, axis=1)
    tile_count = jnp.take_along_axis(range_end - range_start, owner_index, axis=1)
    offset_inside = position[None, :] - first_tile
    head_count = tile_count - SPILL
    head_blocks = BPD - SPILL
    in_head = offset_inside < head_count
    head_block = offset_inside * head_blocks // head_count
    head_rank = offset_inside - (head_block * head_count + head_blocks - 1) // head_blocks
    tail_index = offset_inside - head_count
    block_inside = jnp.where(in_head, head_block, head_blocks + tail_index)
    groups = jnp.arange(N_GRP, dtype=jnp.int32)[:, None]
    owner_first = groups * (N_DEV * BPD) + owner_index * BPD
    row_blocks = owner_first + block_inside
    offset_draw = jax.random.randint(offset_key, row_blocks.shape, -R, R + 1)
    head_offset = jnp.where(head_rank == 0, 0, jnp.where(head_rank == 1, -R, jnp.where(head_rank == 2, R, offset_draw)))
    tail_offset = jnp.where(tail_index % 2 == 0, -R, offset_draw)
    head_cols = jnp.clip(row_blocks + head_offset, 0, device_count * BPD - 1)
    tail_cols = jnp.clip(jnp.maximum(row_blocks + tail_offset, owner_first), 0, device_count * BPD - 1)
    col_blocks = jnp.where(in_head, head_cols, tail_cols)
    return (row_blocks.reshape(-1).astype(jnp.int32), col_blocks.reshape(-1).astype(jnp.int32))


def column_pattern(key):
    device_count = N_GRP * N_DEV
    level_key = jax.random.fold_in(key, 21)
    order_key = jax.random.fold_in(key, 22)
    shuffle_key = jax.random.fold_in(key, 23)
    levels = jax.random.randint(level_key, (device_count, COLS_DEV), 1, LEV + 1)
    column_ids = jnp.arange(COLS_DEV, dtype=jnp.int32)
    levels = jnp.where(column_ids[None, :] == 0, LEV, jnp.where(column_ids[None, :] == 1, 1, levels))
    tie_break = jnp.argsort(jax.random.randint(order_key, (device_count, COLS_DEV), 0, 2 ** 30), axis=1, stable=True)
    depth_score = levels * COLS_DEV + tie_break
    depth_rank = jnp.argsort(jnp.argsort(-depth_score, axis=1, stable=True), axis=1, stable=True)
    band_index = depth_rank // N_DEV
    place_index = depth_rank % N_DEV
    slot_index = jnp.where(band_index % 2 == 0, place_index, N_DEV - 1 - place_index)
    shuffle = jnp.argsort(jax.random.randint(shuffle_key, (device_count, N_DEV), 0, 2 ** 30), axis=1, stable=True)
    owner_index = jnp.take_along_axis(shuffle, slot_index, axis=1)
    return (levels.reshape(-1).astype(jnp.int32), owner_index.reshape(-1).astype(jnp.int32))


def draw_tile_rows(key, part):
    return tile_pattern(key)[0]


def draw_tile_cols(key, part):
    return tile_pattern(key)[1]


def draw_level_counts(key, part):
    return column_pattern(key)[0]


def draw_column_owner(key, part):
    return column_pattern(key)[1]


def block_scale(own_key, dims, cuts, least, high):
    gain = 1.0
    for dim, shards_of in cuts:
        draws = jax.random.uniform(jax.random.fold_in(jax.random.fold_in(own_key, 6), dim), (shards_of,), jnp.float32, least / len(cuts), high / len(cuts))
        gain = gain * jnp.repeat(jnp.exp(draws), dims[dim] // shards_of).reshape((-1,) + (1,) * (len(dims) - 1 - dim))
    return gain


def gaussian(own_key, extent, width, most, pieces=(), held_as=jnp.bfloat16):
    result = width * jax.random.normal(own_key, extent, jnp.float32)
    if pieces:
        result = result * block_scale(own_key, extent, pieces, -0.22, 0.18)
    return jnp.clip(result, -most, most).astype(held_as)


def setup_inputs(seed: int = 0) -> dict:
    key_of = jax.random.split(jax.random.key(seed), 12)
    return {
        "tracer": jnp.clip(0.05 + 1.95 * jax.random.uniform(key_of[0], (NTR, NCELL), jnp.float32) ** block_scale(key_of[0], (NTR, NCELL), ((1, 32),), -0.2, 0.2), 0.05, 2.0),
        "tile_rows": draw_tile_rows(jax.random.fold_in(key_of[11], 71), 0),
        "tile_cols": draw_tile_cols(jax.random.fold_in(key_of[11], 71), 0),
        "tile_values": gaussian(key_of[3], (TILES, BLK, BLK), (TPB * BLK) ** -0.5, 0.25, ((0, 32),)),
        "level_counts": draw_level_counts(jax.random.fold_in(key_of[11], 71), 0),
        "column_owner": draw_column_owner(jax.random.fold_in(key_of[11], 71), 0),
        "half_saturation": jnp.clip(jnp.exp(jax.random.uniform(key_of[6], (NUT,), jnp.float32, math.log(0.1), math.log(1.0))), 0.1, 1.0),
        "growth_rate": jnp.clip(jnp.exp(jax.random.uniform(key_of[7], (PLK,), jnp.float32, math.log(0.2), math.log(2.0))), 0.2, 2.0),
        "uptake": jnp.clip(jax.random.uniform(key_of[8], (PLK, NUT), jnp.float32, 0.0, 0.125), 0.0, 0.125),
        "graze_preference": jnp.clip(jax.random.uniform(key_of[9], (PLK, PLK), jnp.float32, 0.0, 0.03125), 0.0, 0.03125),
        "graze_maximum": jnp.clip(jnp.exp(jax.random.uniform(key_of[10], (PLK,), jnp.float32, math.log(0.2), math.log(2.0))), 0.2, 2.0),
    }


highest = lax.Precision.HIGHEST
WATER_DECAY = 0.03
SHADE_DECAY = 0.05
EFFICIENCY = 0.3
MORTALITY = 0.1
REMINERAL = 0.2
TIMESTEP = 0.5


def ecosystem(cells, levels, half_saturation, growth_rate, uptake, graze_preference, graze_maximum):
    column_count = levels.shape[0]
    depth_index = lax.broadcasted_iota(jnp.int32, (column_count, LEV), 1).astype(jnp.float32)
    wet_mask = (depth_index < levels[:, None]).astype(jnp.float32).reshape(1, column_count * LEV)
    nutrient = cells[:NUT]
    plankton = cells[NUT:NUT + PLK]
    detritus = cells[NUT + PLK:]
    chlorophyll = (jnp.sum(plankton, axis=0, keepdims=True) / PLK * wet_mask).reshape(column_count, LEV)
    above_mask = (lax.broadcasted_iota(jnp.int32, (LEV, LEV), 0) < lax.broadcasted_iota(jnp.int32, (LEV, LEV), 1)).astype(jnp.float32)
    shading = jnp.dot(chlorophyll, above_mask, precision=highest).reshape(1, column_count * LEV)
    sunlight = jnp.exp(-WATER_DECAY * depth_index.reshape(1, column_count * LEV) - SHADE_DECAY * shading)
    monod_term = nutrient / (nutrient + half_saturation[:, None])
    limitation = jnp.dot(uptake, monod_term, precision=highest)
    capacity = growth_rate[:, None] * sunlight * plankton
    growth = capacity * limitation
    food_sum = jnp.dot(graze_preference, plankton, precision=highest)
    graze_rate = graze_maximum[:, None] * plankton / (1.0 + food_sum)
    grazed = plankton * jnp.dot(graze_preference.T, graze_rate, precision=highest)
    eaten_total = graze_rate * food_sum
    d_plankton = growth - grazed + EFFICIENCY * eaten_total - MORTALITY * plankton
    d_nutrient = -monod_term * jnp.dot(uptake.T, capacity, precision=highest) + REMINERAL * detritus
    waste_flux = ((1.0 - EFFICIENCY) * eaten_total + MORTALITY * plankton).reshape(NUT, PLK // NUT, column_count * LEV)
    d_detritus = jnp.sum(waste_flux, axis=1) - REMINERAL * detritus
    source = jnp.concatenate([d_nutrient, d_plankton, d_detritus], axis=0) * wet_mask
    column_sum = jnp.sum((jnp.sum(growth, axis=0) / PLK * wet_mask[0]).reshape(column_count, LEV), axis=1)
    return source, column_sum


def reference(tracer, tile_rows, tile_cols, tile_values, level_counts, column_owner, half_saturation, growth_rate, uptake, graze_preference, graze_maximum):
    device_count = N_GRP * N_DEV
    block_count = device_count * BPD
    coarse = lax.optimization_barrier(tracer.astype(jnp.bfloat16))
    blocks = coarse.astype(jnp.float32).reshape(NTR, block_count, BLK).transpose(1, 0, 2)
    row_blocks = tile_rows.reshape(device_count, NT)
    col_blocks = tile_cols.reshape(device_count, NT)
    tile_data = tile_values.reshape(device_count, NT, BLK, BLK)

    def add_device(running, tile_batch):
        batch_rows, batch_cols, batch_data = tile_batch
        picked = blocks[batch_cols]
        contrib = jnp.einsum("tcb,tab->tca", picked, batch_data.astype(jnp.float32), precision=highest)
        return running.at[batch_rows].add(contrib), None

    running, _ = lax.scan(add_device, jnp.zeros((block_count, NTR, BLK), jnp.float32), (row_blocks, col_blocks, tile_data))
    transport = running.transpose(1, 0, 2).reshape(NTR, block_count * BLK)

    shards = tracer.reshape(NTR, device_count, CD).transpose(1, 0, 2)
    shard_levels = level_counts.reshape(device_count, COLS_DEV).astype(jnp.float32)

    def one_device(pair):
        return ecosystem(pair[0], pair[1], half_saturation, growth_rate, uptake, graze_preference, graze_maximum)

    sources, column_sums = lax.map(one_device, (shards, shard_levels))
    source = sources.transpose(1, 0, 2).reshape(NTR, device_count * CD)
    updated = tracer + transport + TIMESTEP * source

    owners = column_owner.reshape(N_GRP, N_DEV, COLS_DEV)
    send_order = jnp.argsort(owners, axis=2, stable=True).astype(jnp.int32)
    sorted_sums = jnp.take_along_axis(column_sums.reshape(N_GRP, N_DEV, COLS_DEV), send_order, axis=2)
    production = sorted_sums.reshape(N_GRP, N_DEV, N_DEV, COLS_DEV // N_DEV).transpose(0, 2, 1, 3).reshape(N_GRP * N_DEV * COLS_DEV)
    return updated, production
```

```python
import jax
import jax.numpy as jnp
from jax import lax
from jax.experimental import pallas as pl
from jax.experimental.pallas import tpu as pltpu
from jax.sharding import PartitionSpec as P

NUT = 16
PLK = 64
LEV = 32
REACH = 16
LANES = 128
CHUNK = 256

HIGHEST = lax.Precision.HIGHEST
WATER_DECAY = 0.03
SHADE_DECAY = 0.05
EFFICIENCY = 0.3
MORTALITY = 0.1
REMINERAL = 0.2
TIMESTEP = 0.5
F32 = jnp.float32
BF16 = jnp.bfloat16
CHAIN = ("grp", "dev")


def chain_shift(x, step):
    count = lax.axis_size(CHAIN)
    pairs = [(i, i + step) for i in range(count) if 0 <= i + step < count]
    return lax.ppermute(x, CHAIN, pairs)


def group_shift(x, step):
    count = lax.axis_size("dev")
    pairs = [(i, i + step) for i in range(count) if 0 <= i + step < count]
    return lax.ppermute(x, "dev", pairs)


def iota(shape, dim):
    return lax.broadcasted_iota(jnp.int32, shape, dim)


def rows_dot(a, b, precision=None):
    return lax.dot_general(
        a, b, (((1,), (1,)), ((), ())), precision=precision, preferred_element_type=F32
    )


def dot(a, b, precision=None):
    return jnp.dot(a, b, precision=precision, preferred_element_type=F32)


def round_kernel(x_ref, out_ref):
    out_ref[...] = x_ref[...].astype(BF16)


def rounded(x, start, width, parts=2):
    rows, piece = x.shape[0], width // parts
    return pl.pallas_call(
        round_kernel,
        out_shape=jax.ShapeDtypeStruct((rows, width), BF16),
        grid=(parts,),
        in_specs=[pl.BlockSpec((rows, piece), lambda i: (0, start // piece + i))],
        out_specs=pl.BlockSpec((rows, piece), lambda i: (0, i)),
        compiler_params=pltpu.CompilerParams(vmem_limit_bytes=4 << 20),
        cost_estimate=pl.CostEstimate(
            flops=rows * width, bytes_accessed=rows * width * 6, transcendentals=0
        ),
    )(x)


def ecosystem_kernel(
    x_ref, tiles_ref, rows_ref, cols_ref, level_ref, owner_ref, half_ref, rate_ref,
    uptake_ref, prefer_ref, graze_ref, after_low_ref, after_high_ref,
    base_ref, send_ref, more_ref, index_ref, light_ref, wet_ref, sums_ref, sem,
):
    spill = pltpu.make_async_copy(tiles_ref.at[pl.ds(0, more_ref.shape[0])], more_ref, sem)
    spill.start()
    index_ref[0:1, :] = rows_ref[:, :LANES]
    index_ref[1:2, :] = cols_ref[:, :LANES]
    blocks = x_ref.shape[1] // LANES
    per_block = LANES // LEV
    columns = level_ref.shape[1]
    devices = send_ref.shape[0]

    mine = iota((blocks, columns), 1) // per_block == iota((blocks, columns), 0)
    spread = (
        iota((columns, LANES), 0) % per_block == iota((columns, LANES), 1) // LEV
    ).astype(F32)
    levels = level_ref[...].astype(F32)
    counts = dot(jnp.where(mine, levels, 0.0), spread, HIGHEST)
    depth = (iota((blocks, LANES), 1) % LEV).astype(F32)
    wet = (depth < counts).astype(F32)
    wet_ref[...] = wet

    for i in range(blocks):
        plankton = x_ref[NUT : NUT + PLK, i * LANES : (i + 1) * LANES]
        sums_ref[i : i + 1, :] = jnp.sum(plankton, axis=0, keepdims=True)
    upper, lower = iota((LANES, LANES), 0), iota((LANES, LANES), 1)
    above = ((upper // LEV == lower // LEV) & (upper < lower)).astype(F32)
    shading = dot(sums_ref[...] / PLK * wet, above, HIGHEST)
    light_ref[...] = jnp.exp(-WATER_DECAY * depth - SHADE_DECAY * shading)

    def upright(ref):
        n = ref.shape[1]
        return jnp.sum(
            jnp.where(iota((n, n), 0) == iota((n, n), 1), ref[...], 0.0), axis=1, keepdims=True
        )

    half = upright(half_ref)
    rate = upright(rate_ref)
    most = upright(graze_ref)
    prefer = prefer_ref[...]
    uptake = uptake_ref[...].T
    prefer_b = prefer.astype(BF16)
    prefer_t = prefer.T.astype(BF16)
    uptake_b = uptake.astype(BF16)
    uptake_t = uptake_ref[...].astype(BF16)
    quarter = (iota((NUT, PLK), 1) // (PLK // NUT) == iota((NUT, PLK), 0)).astype(BF16)
    span = CHUNK // LANES

    def row_of(ref, k):
        return jnp.concatenate([ref[pl.ds(k * span + s, 1), :] for s in range(span)], axis=1)

    def step(k, carry):
        at = pl.ds(pl.multiple_of(k * CHUNK, CHUNK), CHUNK)
        nutrient = x_ref[:NUT, at]
        plankton = x_ref[NUT : NUT + PLK, at]
        detritus = x_ref[NUT + PLK :, at]
        sun = row_of(light_ref, k)
        mask = row_of(wet_ref, k)
        monod = nutrient / (nutrient + half)
        limitation = dot(uptake_b, monod.astype(BF16))
        capacity = rate * sun * plankton
        growth = capacity * limitation
        food = dot(prefer_b, plankton.astype(BF16))
        graze = most * plankton / (1.0 + food)
        grazed = plankton * dot(prefer_t, graze.astype(BF16))
        eaten = graze * food
        d_plankton = growth - grazed + EFFICIENCY * eaten - MORTALITY * plankton
        d_nutrient = -monod * dot(uptake_t, capacity.astype(BF16)) + REMINERAL * detritus
        waste = (1.0 - EFFICIENCY) * eaten + MORTALITY * plankton
        waste_high = waste.astype(BF16)
        waste_low = (waste - waste_high.astype(F32)).astype(BF16)
        d_detritus = dot(quarter, waste_high) + dot(quarter, waste_low) - REMINERAL * detritus
        scale = TIMESTEP * mask
        base_ref[:NUT, at] = nutrient + scale * d_nutrient
        base_ref[NUT : NUT + PLK, at] = plankton + scale * d_plankton
        base_ref[NUT + PLK :, at] = detritus + scale * d_detritus
        total = jnp.sum(growth, axis=0, keepdims=True) / PLK * mask
        for s in range(span):
            sums_ref[pl.ds(k * span + s, 1), :] = total[:, s * LANES : (s + 1) * LANES]
        return carry

    lax.fori_loop(0, x_ref.shape[1] // CHUNK, step, 0)

    by_column = dot(sums_ref[...], spread.T, HIGHEST)
    production = jnp.sum(jnp.where(mine, by_column, 0.0), axis=0, keepdims=True)
    owned = owner_ref[...] == iota((devices, columns), 0)
    before = (iota((columns, columns), 0) < iota((columns, columns), 1)).astype(BF16)
    earlier = dot(owned.astype(BF16), before)
    rank = jnp.sum(jnp.where(owned, earlier, 0.0), axis=0, keepdims=True).astype(jnp.int32)
    place = (rank == iota((LANES, columns), 0)).astype(F32)
    send_ref[...] = rows_dot(jnp.where(owned, production, 0.0), place, HIGHEST)
    spill.wait()


def tiles_kernel(index_ref, tiles_ref, low_ref, high_ref, left_ref, right_ref,
                 base_ref, out_ref, near_ref, held_ref, sems):
    blocks = base_ref.shape[1] // LANES
    half = blocks // 2
    width = half * LANES
    pieces = sems.shape[0]
    batch = held_ref.shape[0] // pieces
    first = (lax.axis_index("grp") * lax.axis_size("dev") + lax.axis_index("dev")) * blocks

    def load(k):
        at = pl.ds(k * batch, batch)
        return pltpu.make_async_copy(tiles_ref.at[at], held_ref.at[at], sems.at[k])

    for k in range(pieces):
        load(k).start()
    out_ref[...] = base_ref[...]
    for k, ref in enumerate((left_ref, low_ref, high_ref, right_ref)):
        near_ref[:, k * width : (k + 1) * width] = ref[...]

    def piece(k, carry):
        load(k).wait()
        for j in range(batch):
            t = k * batch + j
            slot = index_ref[0, t] - first
            mine = (slot >= 0) & (slot < blocks)
            slot = jnp.clip(slot, 0, blocks - 1)
            col = jnp.clip(index_ref[1, t] - first + half, 0, 4 * half - 1)
            cells = near_ref[:, pl.ds(pl.multiple_of(col * LANES, LANES), LANES)]
            part = rows_dot(cells, held_ref[t])
            at = pl.ds(pl.multiple_of(slot * LANES, LANES), LANES)
            out_ref[:, at] += jnp.where(mine, part, 0.0)
        return carry

    lax.fori_loop(0, pieces, piece, 0)


def call_tiles(index, tiles, low, high, left, right, base, batch, space):
    count, size = tiles.shape[0], tiles.shape[1]
    channels, cells = base.shape
    whole = lambda a: pl.BlockSpec(a.shape, lambda i, *_: (0, 0))
    return pl.pallas_call(
        tiles_kernel,
        out_shape=jax.ShapeDtypeStruct(base.shape, F32),
        grid_spec=pltpu.PrefetchScalarGridSpec(
            num_scalar_prefetch=1,
            grid=(1,),
            in_specs=[pl.BlockSpec(memory_space=space)]
            + [whole(a) for a in (low, high, left, right, base)],
            out_specs=whole(base),
            scratch_shapes=[
                pltpu.VMEM((channels, 2 * cells), BF16),
                pltpu.VMEM((count, size, size), BF16),
                pltpu.SemaphoreType.DMA((count // batch,)),
            ],
        ),
        compiler_params=pltpu.CompilerParams(vmem_limit_bytes=24 << 20),
        cost_estimate=pl.CostEstimate(
            flops=2 * count * channels * size * size,
            bytes_accessed=tiles.size * 2 + base.size * 12,
            transcendentals=0,
        ),
    )(index, tiles, low, high, left, right, base)


def per_device(
    tracer, tile_rows, tile_cols, tile_values, level_counts, column_owner,
    half_saturation, growth_rate, uptake, graze_preference, graze_maximum,
):
    channels, cells = tracer.shape
    tile_total, block = tile_values.shape[0], tile_values.shape[1]
    spill = tile_total // 8
    half = cells // 2
    assert half >= REACH * block and block == LANES
    devices = lax.axis_size("dev")

    high = rounded(tracer, half, half)
    low = rounded(tracer, 0, half)
    left = chain_shift(high, 1)
    right = chain_shift(low, -1)

    whole = lambda *shape: pl.BlockSpec(shape, lambda i: (0,) * len(shape))
    base, send, spilled, spilled_index = pl.pallas_call(
        ecosystem_kernel,
        out_shape=(
            jax.ShapeDtypeStruct((channels, cells), F32),
            jax.ShapeDtypeStruct((devices, LANES), F32),
            jax.ShapeDtypeStruct((spill, block, block), BF16),
            jax.ShapeDtypeStruct((2, LANES), jnp.int32),
        ),
        grid=(1,),
        in_specs=[
            whole(channels, cells),
            pl.BlockSpec(memory_space=pltpu.HBM),
            whole(1, tile_total),
            whole(1, tile_total),
            whole(1, level_counts.shape[0]),
            whole(1, column_owner.shape[0]),
            whole(1, NUT),
            whole(1, PLK),
            whole(NUT, PLK),
            whole(PLK, PLK),
            whole(1, PLK),
            pl.BlockSpec(memory_space=pl.ANY),
            pl.BlockSpec(memory_space=pl.ANY),
        ],
        out_specs=(
            whole(channels, cells),
            whole(devices, LANES),
            whole(spill, block, block),
            whole(2, LANES),
        ),
        scratch_shapes=[pltpu.VMEM((cells // LANES, LANES), F32)] * 3 + [pltpu.SemaphoreType.DMA],
        compiler_params=pltpu.CompilerParams(vmem_limit_bytes=20 << 20),
        cost_estimate=pl.CostEstimate(
            flops=cells * 30000, bytes_accessed=channels * cells * 8, transcendentals=cells
        ),
    )(
        tracer,
        tile_values,
        tile_rows[None, :],
        tile_cols[None, :],
        level_counts[None, :],
        column_owner[None, :],
        half_saturation[None, :],
        growth_rate[None, :],
        uptake.T,
        graze_preference,
        graze_maximum[None, :],
        low,
        high,
    )
    share = level_counts.shape[0] // devices
    received = lax.all_to_all(send[:, :share], "dev", split_axis=0, concat_axis=0)
    production = received.reshape(-1)
    more_index = group_shift(spilled_index, -1)
    more_tiles = group_shift(spilled, -1)

    index = jnp.stack([tile_rows, tile_cols])
    mid = call_tiles(index, tile_values, low, high, left, right, base, 16, pltpu.HBM)
    updated = call_tiles(
        more_index, more_tiles, low, high, left, right, mid, spill, pl.ANY
    )
    return updated, production


def solution(mesh):
    return jax.shard_map(
        per_device,
        mesh=mesh,
        in_specs=(
            P(None, CHAIN),
            P(CHAIN),
            P(CHAIN),
            P(CHAIN, None, None),
            P(CHAIN),
            P(CHAIN),
            P(),
            P(),
            P(),
            P(),
            P(),
        ),
        out_specs=(P(None, CHAIN), P(CHAIN)),
        check_vma=False,
    )
```

```python
import functools

import jax
import jax.numpy as jnp
from jax import lax
from jax.experimental import pallas as pl
from jax.experimental.pallas import tpu as pltpu
from jax.sharding import PartitionSpec as P

NUT = 16
PLK = 64
LEV = 32
REACH = 16
LANES = 128
CHUNK = 256

HIGHEST = lax.Precision.HIGHEST
WATER_DECAY = 0.03
SHADE_DECAY = 0.05
EFFICIENCY = 0.3
MORTALITY = 0.1
REMINERAL = 0.2
TIMESTEP = 0.5
F32 = jnp.float32
BF16 = jnp.bfloat16
CHAIN = ("grp", "dev")


def chain_shift(x, step):
    count = lax.axis_size(CHAIN)
    pairs = [(i, i + step) for i in range(count) if 0 <= i + step < count]
    return lax.ppermute(x, CHAIN, pairs)


def group_shift(x, step):
    count = lax.axis_size("dev")
    pairs = [(i, i + step) for i in range(count) if 0 <= i + step < count]
    return lax.ppermute(x, "dev", pairs)


def iota(shape, dim):
    return lax.broadcasted_iota(jnp.int32, shape, dim)


def rows_dot(a, b, precision=None):
    return lax.dot_general(
        a, b, (((1,), (1,)), ((), ())), precision=precision, preferred_element_type=F32
    )


def dot(a, b, precision=None):
    return jnp.dot(a, b, precision=precision, preferred_element_type=F32)


def in_hbm(x):
    return pltpu.with_memory_space_constraint(x, pltpu.HBM)


VMEM_SPEC = pl.BlockSpec(memory_space=pltpu.VMEM)
HBM_SPEC = pl.BlockSpec(memory_space=pltpu.HBM)
ANY_SPEC = pl.BlockSpec(memory_space=pl.ANY)


def round_kernel(start, x_ref, out_ref, held_ref, sems):
    pieces = sems.shape[0]
    width = out_ref.shape[1] // pieces

    def load(k):
        return pltpu.make_async_copy(
            x_ref.at[:, pl.ds(start + k * width, width)],
            held_ref.at[:, pl.ds(k * width, width)],
            sems.at[k],
        )

    for k in range(pieces):
        load(k).start()
    for k in range(pieces):
        load(k).wait()
        at = slice(k * width, (k + 1) * width)
        out_ref[:, at] = held_ref[:, at].astype(BF16)


def rounded(x, start, width, pieces=4):
    rows = x.shape[0]
    return pl.pallas_call(
        functools.partial(round_kernel, start),
        out_shape=jax.ShapeDtypeStruct((rows, width), BF16),
        in_specs=[HBM_SPEC],
        out_specs=VMEM_SPEC,
        scratch_shapes=[pltpu.VMEM((rows, width), F32), pltpu.SemaphoreType.DMA((pieces,))],
        compiler_params=pltpu.CompilerParams(vmem_limit_bytes=4 << 20),
        cost_estimate=pl.CostEstimate(
            flops=rows * width, bytes_accessed=rows * width * 6, transcendentals=0
        ),
    )(x)


def pack_kernel(tiles_ref, rows_ref, cols_ref, after_low_ref, after_high_ref,
                more_ref, index_ref, sem):
    copy = pltpu.make_async_copy(tiles_ref.at[pl.ds(0, more_ref.shape[0])], more_ref, sem)
    copy.start()
    index_ref[0:1, :] = rows_ref[:, :LANES]
    index_ref[1:2, :] = cols_ref[:, :LANES]
    copy.wait()


def ecosystem_kernel(
    x_ref, level_ref, owner_ref, half_ref, rate_ref, uptake_ref, prefer_ref, graze_ref,
    after_ref, far_ref, send_ref, base_ref, light_ref, wet_ref, sums_ref, sem,
):
    blocks = x_ref.shape[1] // LANES
    per_block = LANES // LEV
    columns = level_ref.shape[1]
    devices, _, share = send_ref.shape

    mine = iota((blocks, columns), 1) // per_block == iota((blocks, columns), 0)
    spread = (
        iota((columns, LANES), 0) % per_block == iota((columns, LANES), 1) // LEV
    ).astype(F32)
    levels = level_ref[...].astype(F32)
    counts = dot(jnp.where(mine, levels, 0.0), spread, HIGHEST)
    depth = (iota((blocks, LANES), 1) % LEV).astype(F32)
    wet = (depth < counts).astype(F32)
    wet_ref[...] = wet

    for i in range(blocks):
        plankton = x_ref[NUT : NUT + PLK, i * LANES : (i + 1) * LANES]
        sums_ref[i : i + 1, :] = jnp.sum(plankton, axis=0, keepdims=True)
    upper, lower = iota((LANES, LANES), 0), iota((LANES, LANES), 1)
    above = ((upper // LEV == lower // LEV) & (upper < lower)).astype(F32)
    shading = dot(sums_ref[...] / PLK * wet, above, HIGHEST)
    light_ref[...] = jnp.exp(-WATER_DECAY * depth - SHADE_DECAY * shading)

    def upright(ref):
        n = ref.shape[1]
        return jnp.sum(
            jnp.where(iota((n, n), 0) == iota((n, n), 1), ref[...], 0.0), axis=1, keepdims=True
        )

    half = upright(half_ref)
    rate = upright(rate_ref)
    most = upright(graze_ref)
    prefer = prefer_ref[...]
    uptake = uptake_ref[...].T
    prefer_b = prefer.astype(BF16)
    prefer_t = prefer.T.astype(BF16)
    uptake_b = uptake.astype(BF16)
    uptake_t = uptake_ref[...].astype(BF16)
    quarter = (iota((NUT, PLK), 1) // (PLK // NUT) == iota((NUT, PLK), 0)).astype(BF16)
    span = CHUNK // LANES

    def row_of(ref, k):
        return jnp.concatenate([ref[pl.ds(k * span + s, 1), :] for s in range(span)], axis=1)

    def step(k, carry):
        at = pl.ds(pl.multiple_of(k * CHUNK, CHUNK), CHUNK)
        nutrient = x_ref[:NUT, at]
        plankton = x_ref[NUT : NUT + PLK, at]
        detritus = x_ref[NUT + PLK :, at]
        sun = row_of(light_ref, k)
        mask = row_of(wet_ref, k)
        monod = nutrient / (nutrient + half)
        limitation = dot(uptake_b, monod.astype(BF16))
        capacity = rate * sun * plankton
        growth = capacity * limitation
        food = dot(prefer_b, plankton.astype(BF16))
        graze = most * plankton / (1.0 + food)
        grazed = plankton * dot(prefer_t, graze.astype(BF16))
        eaten = graze * food
        d_plankton = growth - grazed + EFFICIENCY * eaten - MORTALITY * plankton
        d_nutrient = -monod * dot(uptake_t, capacity.astype(BF16)) + REMINERAL * detritus
        waste = (1.0 - EFFICIENCY) * eaten + MORTALITY * plankton
        waste_high = waste.astype(BF16)
        waste_low = (waste - waste_high.astype(F32)).astype(BF16)
        d_detritus = dot(quarter, waste_high) + dot(quarter, waste_low) - REMINERAL * detritus
        scale = TIMESTEP * mask
        base_ref[:NUT, at] = nutrient + scale * d_nutrient
        base_ref[NUT : NUT + PLK, at] = plankton + scale * d_plankton
        base_ref[NUT + PLK :, at] = detritus + scale * d_detritus
        total = jnp.sum(growth, axis=0, keepdims=True) / PLK * mask
        for s in range(span):
            sums_ref[pl.ds(k * span + s, 1), :] = total[:, s * LANES : (s + 1) * LANES]
        pltpu.make_async_copy(base_ref.at[:, at], far_ref.at[:, at], sem).start()
        return carry

    lax.fori_loop(0, x_ref.shape[1] // CHUNK, step, 0)

    by_column = dot(sums_ref[...], spread.T, HIGHEST)
    production = jnp.sum(jnp.where(mine, by_column, 0.0), axis=0, keepdims=True)
    owned = owner_ref[...] == iota((devices, columns), 0)
    before = (iota((columns, columns), 0) < iota((columns, columns), 1)).astype(BF16)
    earlier = dot(owned.astype(BF16), before)
    rank = jnp.sum(jnp.where(owned, earlier, 0.0), axis=0, keepdims=True).astype(jnp.int32)
    place = (rank == iota((LANES, columns), 0)).astype(F32)
    sorted_sums = rows_dot(jnp.where(owned, production, 0.0), place, HIGHEST)
    for o in range(devices):
        send_ref[o] = sorted_sums[o : o + 1, :share]
    pltpu.make_async_copy(base_ref, far_ref, sem).wait()


def place_of(index_ref, t, first, held):
    slot = index_ref[0, t] - first
    col = index_ref[1, t] - first
    col = jnp.clip(jnp.where(col < 0, col + held, col), 0, held - 1)
    return slot, pl.ds(pl.multiple_of(col * LANES, LANES), LANES)


def block_at(slot):
    return pl.ds(pl.multiple_of(slot * LANES, LANES), LANES)


def first_block(blocks):
    return (lax.axis_index("grp") * lax.axis_size("dev") + lax.axis_index("dev")) * blocks


def local_kernel(index_ref, tiles_ref, low_ref, high_ref, left_ref, right_ref, base_ref,
                 out_ref, near_ref, reach_ref, held_ref, sems, base_sem, side_sems):
    blocks = base_ref.shape[1] // LANES
    width = low_ref.shape[1]
    pieces = sems.shape[0]
    batch = held_ref.shape[0] // pieces
    first = first_block(blocks)

    def load(k):
        at = pl.ds(k * batch, batch)
        return pltpu.make_async_copy(tiles_ref.at[at], held_ref.at[at], sems.at[k])

    part_of = lambda k: slice(k * width, (k + 1) * width)
    right, left = [
        pltpu.make_async_copy(ref, reach_ref.at[:, part_of(2 + k)], side_sems.at[k])
        for k, ref in enumerate((right_ref, left_ref))
    ]
    right.start()
    left.start()
    start = pltpu.make_async_copy(base_ref, out_ref, base_sem)
    start.start()
    for k in range(pieces):
        load(k).start()
    for k, ref in enumerate((low_ref, high_ref)):
        reach_ref[:, part_of(k)] = ref[...]
        near_ref[:, part_of(k)] = ref[...]
    right.wait()
    near_ref[:, part_of(2)] = reach_ref[:, part_of(2)]
    left.wait()
    start.wait()

    def piece(k, carry):
        load(k).wait()
        for j in range(batch):
            t = k * batch + j
            slot, cells = place_of(index_ref, t, first, 2 * blocks)
            mine = (slot >= 0) & (slot < blocks)
            part = rows_dot(reach_ref[:, cells], held_ref[t])
            out_ref[:, block_at(jnp.clip(slot, 0, blocks - 1))] += jnp.where(mine, part, 0.0)
        return carry

    lax.fori_loop(0, pieces, piece, 0)


def last_kernel(index_ref, tiles_ref, near_ref, mid_ref, received_ref, out_ref, made_ref,
                total_ref, held_ref, sems, out_sem):
    blocks = mid_ref.shape[1] // LANES
    pieces = sems.shape[0]
    batch = held_ref.shape[0] // pieces
    first = first_block(blocks)

    def load(k):
        at = pl.ds(k * batch, batch)
        return pltpu.make_async_copy(tiles_ref.at[at], held_ref.at[at], sems.at[k])

    def store(b, carry):
        at = block_at(b)
        pltpu.make_async_copy(total_ref.at[:, at], out_ref.at[:, at], out_sem).start()
        return carry

    for k in range(pieces):
        load(k).start()
    cells_here = mid_ref.shape[1]
    total_ref[:, :cells_here] = mid_ref[...]
    total_ref[:, cells_here:] = jnp.zeros((mid_ref.shape[0], LANES), F32)
    made_ref[...] = jnp.concatenate(
        [received_ref[o] for o in range(received_ref.shape[0])], axis=1
    )
    done = 0
    for k in range(pieces):
        head = jnp.clip(index_ref[0, k * batch] - first, 0, blocks)
        lax.fori_loop(done, head, store, 0)
        done = jnp.maximum(done, head)
        load(k).wait()
        for t in range(k * batch, (k + 1) * batch):
            slot, cells = place_of(index_ref, t, first, near_ref.shape[1] // LANES)
            slot = jnp.where((slot >= 0) & (slot < blocks), slot, blocks)
            total_ref[:, block_at(slot)] += rows_dot(near_ref[:, cells], held_ref[t])
    lax.fori_loop(done, blocks, store, 0)
    pltpu.make_async_copy(total_ref.at[:, pl.ds(0, cells_here)], out_ref, out_sem).wait()


def per_device(
    tracer, tile_rows, tile_cols, tile_values, level_counts, column_owner,
    half_saturation, growth_rate, uptake, graze_preference, graze_maximum,
):
    channels, cells = tracer.shape
    tile_total, block = tile_values.shape[0], tile_values.shape[1]
    spill = tile_total // 8
    half = cells // 2
    assert half >= REACH * block and block == LANES
    devices = lax.axis_size("dev")

    source = in_hbm(tracer)
    tiles = in_hbm(tile_values)
    high = rounded(source, half, half)
    low = rounded(source, 0, half)
    left = chain_shift(high, 1)
    right = chain_shift(low, -1)

    spilled, spilled_index = pl.pallas_call(
        pack_kernel,
        out_shape=(
            jax.ShapeDtypeStruct((spill, block, block), BF16),
            jax.ShapeDtypeStruct((2, LANES), jnp.int32),
        ),
        in_specs=[HBM_SPEC, VMEM_SPEC, VMEM_SPEC, ANY_SPEC, ANY_SPEC],
        out_specs=(VMEM_SPEC, VMEM_SPEC),
        scratch_shapes=[pltpu.SemaphoreType.DMA],
        compiler_params=pltpu.CompilerParams(vmem_limit_bytes=2 << 20),
        cost_estimate=pl.CostEstimate(
            flops=0, bytes_accessed=spill * block * block * 4, transcendentals=0
        ),
    )(tiles, tile_rows[None, :], tile_cols[None, :], low, high)
    more_index = group_shift(spilled_index, -1)
    more_tiles = group_shift(spilled, -1)

    share = level_counts.shape[0] // devices
    base, send = pl.pallas_call(
        ecosystem_kernel,
        out_shape=(
            pltpu.HBM((channels, cells), F32),
            jax.ShapeDtypeStruct((devices, 1, share), F32),
        ),
        in_specs=[VMEM_SPEC] * 8 + [ANY_SPEC],
        out_specs=(HBM_SPEC, VMEM_SPEC),
        scratch_shapes=[pltpu.VMEM((channels, cells), F32)]
        + [pltpu.VMEM((cells // LANES, LANES), F32)] * 3
        + [pltpu.SemaphoreType.DMA],
        compiler_params=pltpu.CompilerParams(vmem_limit_bytes=4 << 20),
        cost_estimate=pl.CostEstimate(
            flops=cells * 30000, bytes_accessed=channels * cells * 8, transcendentals=cells
        ),
    )(
        tracer,
        level_counts[None, :],
        column_owner[None, :],
        half_saturation[None, :],
        growth_rate[None, :],
        uptake.T,
        graze_preference,
        graze_maximum[None, :],
        spilled,
    )
    received = lax.all_to_all(send, "dev", split_axis=0, concat_axis=0, tiled=True)

    index = jnp.stack([tile_rows, tile_cols])
    smem = pl.BlockSpec(memory_space=pltpu.SMEM)
    pieces = 10
    work = 2 * channels * block * block
    mid, near = pl.pallas_call(
        local_kernel,
        out_shape=(
            jax.ShapeDtypeStruct((channels, cells), F32),
            jax.ShapeDtypeStruct((channels, 3 * half), BF16),
        ),
        in_specs=[smem, HBM_SPEC] + [VMEM_SPEC] * 2 + [HBM_SPEC] * 3,
        out_specs=(VMEM_SPEC, VMEM_SPEC),
        scratch_shapes=[
            pltpu.VMEM((channels, 4 * half), BF16),
            pltpu.VMEM((tile_total, block, block), BF16),
            pltpu.SemaphoreType.DMA((pieces,)),
            pltpu.SemaphoreType.DMA,
            pltpu.SemaphoreType.DMA((2,)),
        ],
        compiler_params=pltpu.CompilerParams(vmem_limit_bytes=8 << 20),
        cost_estimate=pl.CostEstimate(
            flops=tile_total * work, bytes_accessed=tile_values.size * 2, transcendentals=0
        ),
    )(index, tiles, low, high, in_hbm(left), in_hbm(right), in_hbm(base))
    groups = 4
    updated, made = pl.pallas_call(
        last_kernel,
        out_shape=(
            jax.ShapeDtypeStruct((channels, cells), F32),
            jax.ShapeDtypeStruct((1, devices * share), F32),
        ),
        in_specs=[smem, ANY_SPEC, VMEM_SPEC, VMEM_SPEC, VMEM_SPEC],
        out_specs=(HBM_SPEC, VMEM_SPEC),
        scratch_shapes=[
            pltpu.VMEM((channels, cells + LANES), F32),
            pltpu.VMEM((spill, block, block), BF16),
            pltpu.SemaphoreType.DMA((groups,)),
            pltpu.SemaphoreType.DMA,
        ],
        compiler_params=pltpu.CompilerParams(vmem_limit_bytes=8 << 20),
        cost_estimate=pl.CostEstimate(
            flops=spill * work, bytes_accessed=channels * cells * 8, transcendentals=0
        ),
    )(more_index, more_tiles, near, mid, received)
    return updated, made.reshape(-1)


def solution(mesh):
    return jax.shard_map(
        per_device,
        mesh=mesh,
        in_specs=(
            P(None, CHAIN),
            P(CHAIN),
            P(CHAIN),
            P(CHAIN, None, None),
            P(CHAIN),
            P(CHAIN),
            P(),
            P(),
            P(),
            P(),
            P(),
        ),
        out_specs=(P(None, CHAIN), P(CHAIN)),
        check_vma=False,
    )
```

```python
import functools

import jax
import jax.numpy as jnp
from jax import lax
from jax.experimental import pallas as pl
from jax.experimental.pallas import tpu as pltpu
from jax.sharding import PartitionSpec as P

NUT = 16
PLK = 64
LEV = 32
REACH = 16
LANES = 128
CHUNK = 256
SPAN = 512

HIGHEST = lax.Precision.HIGHEST
WATER_DECAY = 0.03
SHADE_DECAY = 0.05
EFFICIENCY = 0.3
MORTALITY = 0.1
REMINERAL = 0.2
TIMESTEP = 0.5
F32 = jnp.float32
BF16 = jnp.bfloat16
CHAIN = ("grp", "dev")


def chain_shift(x, step):
    count = lax.axis_size(CHAIN)
    pairs = [(i, i + step) for i in range(count) if 0 <= i + step < count]
    return lax.ppermute(x, CHAIN, pairs)


def group_shift(x, step):
    count = lax.axis_size("dev")
    pairs = [(i, i + step) for i in range(count) if 0 <= i + step < count]
    return lax.ppermute(x, "dev", pairs)


def iota(shape, dim):
    return lax.broadcasted_iota(jnp.int32, shape, dim)


def rows_dot(a, b, precision=None):
    return lax.dot_general(
        a, b, (((1,), (1,)), ((), ())), precision=precision, preferred_element_type=F32
    )


def dot(a, b, precision=None):
    return jnp.dot(a, b, precision=precision, preferred_element_type=F32)


def in_hbm(x):
    return pltpu.with_memory_space_constraint(x, pltpu.HBM)


VMEM_SPEC = pl.BlockSpec(memory_space=pltpu.VMEM)
HBM_SPEC = pl.BlockSpec(memory_space=pltpu.HBM)
ANY_SPEC = pl.BlockSpec(memory_space=pl.ANY)


def round_kernel(start, x_ref, out_ref, held_ref, sems):
    pieces = sems.shape[0]
    width = out_ref.shape[1] // pieces

    def load(k):
        return pltpu.make_async_copy(
            x_ref.at[:, pl.ds(start + k * width, width)],
            held_ref.at[:, pl.ds(k * width, width)],
            sems.at[k],
        )

    for k in range(pieces):
        load(k).start()
    for k in range(pieces):
        load(k).wait()
        at = slice(k * width, (k + 1) * width)
        out_ref[:, at] = held_ref[:, at].astype(BF16)


def rounded(x, start, width, pieces=4):
    rows = x.shape[0]
    return pl.pallas_call(
        functools.partial(round_kernel, start),
        out_shape=jax.ShapeDtypeStruct((rows, width), BF16),
        in_specs=[HBM_SPEC],
        out_specs=VMEM_SPEC,
        scratch_shapes=[pltpu.VMEM((rows, width), F32), pltpu.SemaphoreType.DMA((pieces,))],
        compiler_params=pltpu.CompilerParams(vmem_limit_bytes=4 << 20),
        cost_estimate=pl.CostEstimate(
            flops=rows * width, bytes_accessed=rows * width * 6, transcendentals=0
        ),
    )(x)


def exact_dot(a, ones):
    n = a.shape[0]
    parts, rest = [], a
    for _ in range(3):
        part = rest.astype(BF16)
        parts.append(part.astype(F32))
        rest = rest - parts[-1]
    out = dot(jnp.concatenate(parts, axis=0).astype(BF16), ones)
    return out[:n] + out[n : 2 * n] + out[2 * n :]


def upright(ref):
    n = ref.shape[1]
    return jnp.sum(
        jnp.where(iota((n, n), 0) == iota((n, n), 1), ref[...], 0.0), axis=1, keepdims=True
    )


def plankton_sent(low_ref, high_ref, c, width):
    half = low_ref.shape[1]
    start = c * width
    ref, at = (low_ref, start) if start < half else (high_ref, start - half)
    return ref[NUT : NUT + PLK, at : at + width]


def produce_kernel(
    x_ref, low_ref, high_ref, level_ref, owner_ref, half_ref, rate_ref, uptake_ref,
    rows_ref, cols_ref, tiles_ref,
    send_ref, lead_ref, rest_ref, light_ref, wet_ref, index_ref, sums_ref, made_ref, held_ref,
    few_ref, more_sem, few_sem,
):
    few = pltpu.make_async_copy(x_ref.at[pl.ds(0, NUT)], few_ref, few_sem)
    few.start()
    lead = lead_ref.shape[0]
    spill = lead + rest_ref.shape[0]
    pack = pltpu.make_async_copy(tiles_ref.at[pl.ds(0, spill)], held_ref, more_sem)
    pack.start()
    cells = x_ref.shape[1]
    blocks = cells // LANES
    slot, col = places(
        rows_ref[...], cols_ref[...], first_block(blocks), blocks, 2 * blocks
    )
    index_ref[0:1, :] = slot
    index_ref[1:2, :] = col
    per_block = LANES // LEV
    columns = level_ref.shape[1]
    devices = send_ref.shape[0]
    share = columns // devices

    half = upright(half_ref)
    weight = jnp.concatenate(
        [uptake_ref[...] * rate_ref[...], jnp.ones((NUT, PLK), F32)], axis=0
    ).astype(BF16)
    few.wait()
    for c in range(cells // SPAN):
        both = dot(weight, plankton_sent(low_ref, high_ref, c, SPAN))
        nutrient = few_ref[:, c * SPAN : (c + 1) * SPAN]
        monod = nutrient / (nutrient + half)
        total = both[NUT : NUT + 1]
        taken = jnp.sum(monod * both[:NUT], axis=0, keepdims=True)
        for s in range(SPAN // LANES):
            row = c * (SPAN // LANES) + s
            sums_ref[row : row + 1, :] = total[:, s * LANES : (s + 1) * LANES]
            made_ref[row : row + 1, :] = taken[:, s * LANES : (s + 1) * LANES]

    pack.wait()
    packs = [
        pltpu.make_async_copy(held_ref.at[pl.ds(0, lead)], lead_ref, more_sem),
        pltpu.make_async_copy(held_ref.at[pl.ds(lead, spill - lead)], rest_ref, few_sem),
    ]
    for pack in packs:
        pack.start()

    mine = iota((blocks, columns), 1) // per_block == iota((blocks, columns), 0)
    spread = iota((columns, LANES), 0) % per_block == iota((columns, LANES), 1) // LEV
    gather = iota((LANES, columns), 1) % per_block == iota((LANES, columns), 0) // LEV
    levels = level_ref[...].astype(F32)
    counts = dot(jnp.where(mine, levels, 0.0).astype(BF16), spread.astype(BF16))
    depth = (iota((blocks, LANES), 1) % LEV).astype(F32)
    wet = (depth < counts).astype(F32)
    wet_ref[...] = wet
    upper, lower = iota((LANES, LANES), 0), iota((LANES, LANES), 1)
    above = ((upper // LEV == lower // LEV) & (upper < lower)).astype(BF16)
    shading = exact_dot(sums_ref[...] / PLK * wet, above)
    light = jnp.exp(-WATER_DECAY * depth - SHADE_DECAY * shading)
    light_ref[...] = light

    by_column = exact_dot(light * made_ref[...] / PLK * wet, gather.astype(BF16))
    production = jnp.sum(jnp.where(mine, by_column, 0.0), axis=0, keepdims=True)
    owned = owner_ref[...] == iota((devices, columns), 0)
    before = (iota((columns, columns), 0) < iota((columns, columns), 1)).astype(BF16)
    earlier = dot(owned.astype(BF16), before)
    rank = jnp.sum(jnp.where(owned, earlier, 0.0), axis=0, keepdims=True).astype(jnp.int32)
    place = (rank == iota((LANES, columns), 0)).astype(F32)
    sorted_sums = rows_dot(jnp.where(owned, production, 0.0), place, HIGHEST)
    lane = iota((1, LANES), 1)
    rows = pltpu.roll(rows_ref[:, :LANES].astype(F32), share, 1)
    cols = pltpu.roll(cols_ref[:, :LANES].astype(F32), share + spill, 1)
    index = jnp.where(lane < share + spill, rows, cols)
    for o in range(devices):
        send_ref[o] = jnp.where(lane < share, sorted_sums[o : o + 1, :], index)
    for pack in packs:
        pack.wait()


def ecosystem_kernel(
    x_ref, low_ref, high_ref, light_ref, wet_ref, half_ref, rate_ref, uptake_ref, prefer_ref,
    graze_ref,
    far_ref, base_ref, held_ref, sem, sems,
):
    cells = x_ref.shape[1]
    pieces = sems.shape[0]
    piece = cells // pieces

    def load(k):
        at = pl.ds(k * piece, piece)
        return pltpu.make_async_copy(x_ref.at[:, at], held_ref.at[:, at], sems.at[k])

    for k in range(pieces):
        load(k).start()
    half = upright(half_ref)
    rate = upright(rate_ref)
    most = upright(graze_ref)
    prefer = prefer_ref[...]
    uptake_b = uptake_ref[...].T.astype(BF16)
    quarter = (iota((NUT, PLK), 1) // (PLK // NUT) == iota((NUT, PLK), 0)).astype(F32)
    first = jnp.concatenate([prefer, uptake_ref[...] * rate_ref[...]], axis=0).astype(BF16)
    second = jnp.concatenate(
        [
            jnp.concatenate([prefer.T, jnp.zeros((PLK, 2 * PLK), F32)], axis=1),
            jnp.concatenate([jnp.zeros((NUT, PLK), F32), quarter, quarter], axis=1),
        ],
        axis=0,
    ).astype(BF16)
    span = CHUNK // LANES

    def row_of(ref, c):
        return jnp.concatenate([ref[c * span + s : c * span + s + 1, :] for s in range(span)], axis=1)

    for c in range(cells // CHUNK):
        if c * CHUNK % piece == 0:
            load(c * CHUNK // piece).wait()
        plankton_b = plankton_sent(low_ref, high_ref, c, CHUNK)
        at = slice(c * CHUNK, (c + 1) * CHUNK)
        nutrient = held_ref[:NUT, at]
        plankton = held_ref[NUT : NUT + PLK, at]
        detritus = held_ref[NUT + PLK :, at]
        sun = row_of(light_ref, c)
        mask = row_of(wet_ref, c)
        both = dot(first, plankton_b)
        food, drawn = both[:PLK], both[PLK:]
        monod = nutrient / (nutrient + half)
        limitation = dot(uptake_b, monod.astype(BF16))
        growth = rate * sun * plankton * limitation
        graze = most * plankton / (1.0 + food)
        eaten = graze * food
        waste = (1.0 - EFFICIENCY) * eaten + MORTALITY * plankton
        waste_high = waste.astype(BF16)
        waste_low = (waste - waste_high.astype(F32)).astype(BF16)
        both = dot(second, jnp.concatenate([graze.astype(BF16), waste_high, waste_low], axis=0))
        lost, fallen = both[:PLK], both[PLK:]
        d_plankton = growth - plankton * lost + EFFICIENCY * eaten - MORTALITY * plankton
        d_nutrient = REMINERAL * detritus - monod * sun * drawn
        d_detritus = fallen - REMINERAL * detritus
        scale = TIMESTEP * mask
        base_ref[:NUT, at] = nutrient + scale * d_nutrient
        base_ref[NUT : NUT + PLK, at] = plankton + scale * d_plankton
        base_ref[NUT + PLK :, at] = detritus + scale * d_detritus
        if c % 4 == 3:
            done = pl.ds((c - 3) * CHUNK, 4 * CHUNK)
            pltpu.make_async_copy(base_ref.at[:, done], far_ref.at[:, done], sem).start()
    pltpu.make_async_copy(base_ref, far_ref, sem).wait()


def places(rows, cols, first, blocks, held):
    slot, col = rows - first, cols - first
    slot = jnp.where((slot >= 0) & (slot < blocks), slot, blocks)
    return slot, jnp.clip(jnp.where(col < 0, col + held, col), 0, held - 1)


def block_at(slot):
    return pl.ds(pl.multiple_of(slot * LANES, LANES), LANES)


def first_block(blocks):
    return (lax.axis_index("grp") * lax.axis_size("dev") + lax.axis_index("dev")) * blocks


def local_kernel(index_ref, tiles_ref, low_ref, high_ref, left_ref, right_ref, base_ref,
                 received_ref, out_ref, picked_ref, slot_ref, made_ref,
                 reach_ref, held_ref, vector_ref, far_ref, sems, base_sem, far_sem):
    cells = base_ref.shape[1]
    blocks = cells // LANES
    width = low_ref.shape[1]
    pieces = sems.shape[0]
    batch = held_ref.shape[0] // pieces
    spill = picked_ref.shape[0]
    devices = received_ref.shape[0]
    share = made_ref.shape[1] // devices

    def load(k):
        at = pl.ds(k * batch, batch)
        return pltpu.make_async_copy(tiles_ref.at[at], held_ref.at[at], sems.at[k])

    me = lax.axis_index("dev")
    row = received_ref[jnp.minimum(me + 1, devices - 1)]
    row = jnp.where(me + 1 < devices, row, -1.0).astype(jnp.int32)
    slot, col = places(row, row, first_block(blocks), blocks, 2 * blocks)
    vector_ref[...] = jnp.where(iota(row.shape, 1) < share + spill, slot, col)
    move = pltpu.make_async_copy(vector_ref, far_ref, far_sem)
    move.start()
    slot_ref[...] = pltpu.roll(slot, LANES - share, 1)
    made_ref[...] = jnp.concatenate(
        [received_ref[o][:, :share] for o in range(devices)], axis=1
    )
    part_of = lambda k: slice(k * width, (k + 1) * width)
    load(0).start()
    start = pltpu.make_async_copy(base_ref, out_ref.at[:, pl.ds(0, cells)], base_sem)
    start.start()
    for k in range(1, pieces):
        load(k).start()
    for k, ref in enumerate((low_ref, high_ref, right_ref, left_ref)):
        reach_ref[:, part_of(k)] = ref[...]
    move.wait()
    for t in range(spill):
        picked_ref[t] = reach_ref[:, block_at(far_ref[0, share + spill + t])]
    out_ref[:, cells:] = jnp.zeros((out_ref.shape[0], LANES), F32)
    start.wait()

    def piece(k, carry):
        load(k).wait()
        for j in range(batch):
            t = k * batch + j
            out_ref[:, block_at(index_ref[0, t])] += rows_dot(
                reach_ref[:, block_at(index_ref[1, t])], held_ref[t]
            )
        return carry

    lax.fori_loop(0, pieces, piece, 0)


def last_kernel(slot_ref, lead_ref, rest_ref, picked_ref, mid_ref, out_ref, total_ref, out_sem):
    cells = out_ref.shape[1]
    blocks = cells // LANES

    def store(b, carry):
        at = block_at(b)
        pltpu.make_async_copy(total_ref.at[:, at], out_ref.at[:, at], out_sem).start()
        return carry

    total_ref[...] = mid_ref[...]
    done, before = 0, 0
    for ref in (lead_ref, rest_ref):
        head = slot_ref[0, before]
        lax.fori_loop(done, head, store, 0)
        done = jnp.maximum(done, head)
        for j in range(ref.shape[0]):
            t = before + j
            total_ref[:, block_at(slot_ref[0, t])] += rows_dot(picked_ref[t], ref[j])
        before += ref.shape[0]
    lax.fori_loop(done, blocks, store, 0)
    pltpu.make_async_copy(total_ref.at[:, pl.ds(0, cells)], out_ref, out_sem).wait()


def per_device(
    tracer, tile_rows, tile_cols, tile_values, level_counts, column_owner,
    half_saturation, growth_rate, uptake, graze_preference, graze_maximum,
):
    channels, cells = tracer.shape
    tile_total, block = tile_values.shape[0], tile_values.shape[1]
    spill = tile_total // 8
    half = cells // 2
    assert half >= REACH * block and block == LANES
    assert level_counts.shape[0] // lax.axis_size("dev") + 2 * spill <= LANES
    devices = lax.axis_size("dev")

    source = in_hbm(tracer)
    tiles = in_hbm(tile_values)
    high = rounded(source, half, half)
    low = rounded(source, 0, half)
    left = chain_shift(high, 1)
    right = chain_shift(low, -1)

    share = level_counts.shape[0] // devices
    blocks = cells // block
    lead = spill // 4
    send, spilled_lead, spilled_rest, light, wet, index = pl.pallas_call(
        produce_kernel,
        out_shape=(
            jax.ShapeDtypeStruct((devices, 1, LANES), F32),
            pltpu.HBM((lead, block, block), BF16),
            pltpu.HBM((spill - lead, block, block), BF16),
            jax.ShapeDtypeStruct((blocks, LANES), F32),
            jax.ShapeDtypeStruct((blocks, LANES), F32),
            jax.ShapeDtypeStruct((2, tile_total), jnp.int32),
        ),
        in_specs=[HBM_SPEC] + [VMEM_SPEC] * 9 + [HBM_SPEC],
        out_specs=(VMEM_SPEC, HBM_SPEC, HBM_SPEC) + (VMEM_SPEC,) * 3,
        scratch_shapes=[
            pltpu.VMEM((blocks, LANES), F32),
            pltpu.VMEM((blocks, LANES), F32),
            pltpu.VMEM((spill, block, block), BF16),
            pltpu.VMEM((NUT, cells), F32),
            pltpu.SemaphoreType.DMA,
            pltpu.SemaphoreType.DMA,
        ],
        compiler_params=pltpu.CompilerParams(vmem_limit_bytes=4 << 20),
        cost_estimate=pl.CostEstimate(
            flops=cells * 8000, bytes_accessed=channels * cells * 4, transcendentals=cells
        ),
    )(
        source,
        low,
        high,
        level_counts[None, :],
        column_owner[None, :],
        half_saturation[None, :],
        growth_rate[None, :],
        uptake.T,
        tile_rows[None, :],
        tile_cols[None, :],
        tiles,
    )
    received = lax.all_to_all(send, "dev", split_axis=0, concat_axis=0, tiled=True)

    lead_tiles = group_shift(spilled_lead, -1)
    rest_tiles = group_shift(spilled_rest, -1)
    base = pl.pallas_call(
        ecosystem_kernel,
        out_shape=pltpu.HBM((channels, cells), F32),
        in_specs=[HBM_SPEC] + [VMEM_SPEC] * 9,
        out_specs=HBM_SPEC,
        scratch_shapes=[pltpu.VMEM((channels, cells), F32)] * 2
        + [pltpu.SemaphoreType.DMA, pltpu.SemaphoreType.DMA((4,))],
        compiler_params=pltpu.CompilerParams(vmem_limit_bytes=4 << 20),
        cost_estimate=pl.CostEstimate(
            flops=cells * 30000, bytes_accessed=channels * cells * 8, transcendentals=0
        ),
    )(
        source,
        low,
        high,
        light,
        wet,
        half_saturation[None, :],
        growth_rate[None, :],
        uptake.T,
        graze_preference,
        graze_maximum[None, :],
    )

    smem = pl.BlockSpec(memory_space=pltpu.SMEM)
    pieces = 10
    work = 2 * channels * block * block
    mid, picked, slots, made = pl.pallas_call(
        local_kernel,
        out_shape=(
            jax.ShapeDtypeStruct((channels, cells + LANES), F32),
            jax.ShapeDtypeStruct((spill, channels, block), BF16),
            jax.ShapeDtypeStruct((1, LANES), jnp.int32),
            jax.ShapeDtypeStruct((1, devices * share), F32),
        ),
        in_specs=[smem, HBM_SPEC] + [VMEM_SPEC] * 4 + [HBM_SPEC, VMEM_SPEC],
        out_specs=(VMEM_SPEC,) * 4,
        scratch_shapes=[
            pltpu.VMEM((channels, 4 * half), BF16),
            pltpu.VMEM((tile_total, block, block), BF16),
            pltpu.VMEM((1, LANES), jnp.int32),
            pltpu.SMEM((1, LANES), jnp.int32),
            pltpu.SemaphoreType.DMA((pieces,)),
            pltpu.SemaphoreType.DMA,
            pltpu.SemaphoreType.DMA,
        ],
        compiler_params=pltpu.CompilerParams(vmem_limit_bytes=10 << 20),
        cost_estimate=pl.CostEstimate(
            flops=tile_total * work, bytes_accessed=tile_values.size * 2, transcendentals=0
        ),
    )(index, tiles, low, high, left, right, in_hbm(base), received)
    updated = pl.pallas_call(
        last_kernel,
        out_shape=jax.ShapeDtypeStruct((channels, cells), F32),
        in_specs=[smem] + [VMEM_SPEC] * 4,
        out_specs=HBM_SPEC,
        scratch_shapes=[
            pltpu.VMEM((channels, cells + LANES), F32),
            pltpu.SemaphoreType.DMA,
        ],
        compiler_params=pltpu.CompilerParams(vmem_limit_bytes=6 << 20),
        cost_estimate=pl.CostEstimate(
            flops=spill * work, bytes_accessed=channels * cells * 8, transcendentals=0
        ),
    )(slots, lead_tiles, rest_tiles, picked, mid)
    return updated, made.reshape(-1)


def solution(mesh):
    return jax.shard_map(
        per_device,
        mesh=mesh,
        in_specs=(
            P(None, CHAIN),
            P(CHAIN),
            P(CHAIN),
            P(CHAIN, None, None),
            P(CHAIN),
            P(CHAIN),
            P(),
            P(),
            P(),
            P(),
            P(),
        ),
        out_specs=(P(None, CHAIN), P(CHAIN)),
        check_vma=False,
    )
```

```python
import functools

import jax
import jax.numpy as jnp
from jax import lax
from jax.experimental import pallas as pl
from jax.experimental.pallas import tpu as pltpu
from jax.sharding import PartitionSpec as P

NUT = 16
PLK = 64
LEV = 32
REACH = 16
LANES = 128
CHUNK = 256
SPAN = 512

HIGHEST = lax.Precision.HIGHEST
WATER_DECAY = 0.03
SHADE_DECAY = 0.05
EFFICIENCY = 0.3
MORTALITY = 0.1
REMINERAL = 0.2
TIMESTEP = 0.5
F32 = jnp.float32
BF16 = jnp.bfloat16
CHAIN = ("grp", "dev")


def chain_shift(x, step):
    count = lax.axis_size(CHAIN)
    pairs = [(i, i + step) for i in range(count) if 0 <= i + step < count]
    return lax.ppermute(x, CHAIN, pairs)


def group_shift(x, step):
    count = lax.axis_size("dev")
    pairs = [(i, i + step) for i in range(count) if 0 <= i + step < count]
    return lax.ppermute(x, "dev", pairs)


def iota(shape, dim):
    return lax.broadcasted_iota(jnp.int32, shape, dim)


def rows_dot(a, b, precision=None):
    return lax.dot_general(
        a, b, (((1,), (1,)), ((), ())), precision=precision, preferred_element_type=F32
    )


def dot(a, b, precision=None):
    return jnp.dot(a, b, precision=precision, preferred_element_type=F32)


def in_hbm(x):
    return pltpu.with_memory_space_constraint(x, pltpu.HBM)


VMEM_SPEC = pl.BlockSpec(memory_space=pltpu.VMEM)
HBM_SPEC = pl.BlockSpec(memory_space=pltpu.HBM)
ANY_SPEC = pl.BlockSpec(memory_space=pl.ANY)


def round_kernel(start, x_ref, out_ref, held_ref, sems):
    pieces = sems.shape[0]
    rows, width = out_ref.shape[0] // pieces, out_ref.shape[1]

    def load(k):
        at = pl.ds(k * rows, rows)
        return pltpu.make_async_copy(
            x_ref.at[at, pl.ds(start, width)], held_ref.at[at], sems.at[k]
        )

    for k in range(pieces):
        load(k).start()
    for k in range(pieces):
        load(k).wait()
        at = slice(k * rows, (k + 1) * rows)
        out_ref[at, :] = held_ref[at, :].astype(BF16)


def rounded(x, start, width, pieces=3):
    rows = x.shape[0]
    return pl.pallas_call(
        functools.partial(round_kernel, start),
        out_shape=jax.ShapeDtypeStruct((rows, width), BF16),
        in_specs=[HBM_SPEC],
        out_specs=VMEM_SPEC,
        scratch_shapes=[pltpu.VMEM((rows, width), F32), pltpu.SemaphoreType.DMA((pieces,))],
        compiler_params=pltpu.CompilerParams(vmem_limit_bytes=4 << 20),
        cost_estimate=pl.CostEstimate(
            flops=rows * width, bytes_accessed=rows * width * 6, transcendentals=0
        ),
    )(x)


def exact_dot(a, ones):
    n = a.shape[0]
    parts, rest = [], a
    for _ in range(3):
        part = rest.astype(BF16)
        parts.append(part.astype(F32))
        rest = rest - parts[-1]
    out = dot(jnp.concatenate(parts, axis=0).astype(BF16), ones)
    return out[:n] + out[n : 2 * n] + out[2 * n :]


def upright(ref):
    n = ref.shape[1]
    return jnp.sum(
        jnp.where(iota((n, n), 0) == iota((n, n), 1), ref[...], 0.0), axis=1, keepdims=True
    )


def plankton_sent(low_ref, high_ref, c, width):
    half = low_ref.shape[1]
    start = c * width
    ref, at = (low_ref, start) if start < half else (high_ref, start - half)
    return ref[NUT : NUT + PLK, at : at + width]


def produce_kernel(
    x_ref, low_ref, high_ref, level_ref, owner_ref, half_ref, rate_ref, uptake_ref,
    rows_ref, cols_ref, tiles_ref,
    send_ref, more_ref, light_ref, wet_ref, index_ref, sums_ref, made_ref, held_ref,
    few_ref, more_sem, few_sem,
):
    few = pltpu.make_async_copy(x_ref.at[pl.ds(0, NUT)], few_ref, few_sem)
    few.start()
    spill = more_ref.shape[0]
    pack = pltpu.make_async_copy(tiles_ref.at[pl.ds(0, spill)], held_ref, more_sem)
    pack.start()
    cells = x_ref.shape[1]
    blocks = cells // LANES
    slot, col = places(
        rows_ref[...], cols_ref[...], first_block(blocks), blocks, 2 * blocks
    )
    index_ref[0:1, :] = slot
    index_ref[1:2, :] = col
    per_block = LANES // LEV
    columns = level_ref.shape[1]
    devices = send_ref.shape[0]
    share = columns // devices

    half = upright(half_ref)
    weight = jnp.concatenate(
        [uptake_ref[...] * rate_ref[...], jnp.ones((NUT, PLK), F32)], axis=0
    ).astype(BF16)
    few.wait()
    for c in range(cells // SPAN):
        both = dot(weight, plankton_sent(low_ref, high_ref, c, SPAN))
        nutrient = few_ref[:, c * SPAN : (c + 1) * SPAN]
        monod = nutrient / (nutrient + half)
        total = both[NUT : NUT + 1]
        taken = jnp.sum(monod * both[:NUT], axis=0, keepdims=True)
        for s in range(SPAN // LANES):
            row = c * (SPAN // LANES) + s
            sums_ref[row : row + 1, :] = total[:, s * LANES : (s + 1) * LANES]
            made_ref[row : row + 1, :] = taken[:, s * LANES : (s + 1) * LANES]

    pack.wait()
    pack = pltpu.make_async_copy(held_ref, more_ref, more_sem)
    pack.start()

    mine = iota((blocks, columns), 1) // per_block == iota((blocks, columns), 0)
    spread = iota((columns, LANES), 0) % per_block == iota((columns, LANES), 1) // LEV
    gather = iota((LANES, columns), 1) % per_block == iota((LANES, columns), 0) // LEV
    levels = level_ref[...].astype(F32)
    counts = dot(jnp.where(mine, levels, 0.0).astype(BF16), spread.astype(BF16))
    depth = (iota((blocks, LANES), 1) % LEV).astype(F32)
    wet = (depth < counts).astype(F32)
    wet_ref[...] = wet
    upper, lower = iota((LANES, LANES), 0), iota((LANES, LANES), 1)
    above = ((upper // LEV == lower // LEV) & (upper < lower)).astype(BF16)
    shading = exact_dot(sums_ref[...] / PLK * wet, above)
    light = jnp.exp(-WATER_DECAY * depth - SHADE_DECAY * shading)
    light_ref[...] = light

    by_column = exact_dot(light * made_ref[...] / PLK * wet, gather.astype(BF16))
    production = jnp.sum(jnp.where(mine, by_column, 0.0), axis=0, keepdims=True)
    owned = owner_ref[...] == iota((devices, columns), 0)
    before = (iota((columns, columns), 0) < iota((columns, columns), 1)).astype(BF16)
    earlier = dot(owned.astype(BF16), before)
    rank = jnp.sum(jnp.where(owned, earlier, 0.0), axis=0, keepdims=True).astype(jnp.int32)
    place = (rank == iota((LANES, columns), 0)).astype(F32)
    sorted_sums = rows_dot(jnp.where(owned, production, 0.0), place, HIGHEST)
    lane = iota((1, LANES), 1)
    rows = pltpu.roll(rows_ref[:, :LANES].astype(F32), share, 1)
    cols = pltpu.roll(cols_ref[:, :LANES].astype(F32), share + spill, 1)
    index = jnp.where(lane < share + spill, rows, cols)
    for o in range(devices):
        send_ref[o] = jnp.where(lane < share, sorted_sums[o : o + 1, :], index)
    pack.wait()


def ecosystem_kernel(
    x_ref, low_ref, high_ref, light_ref, wet_ref, half_ref, rate_ref, uptake_ref, prefer_ref,
    graze_ref,
    far_ref, base_ref, held_ref, sem, sems,
):
    cells = x_ref.shape[1]
    pieces = sems.shape[0]
    piece = cells // pieces

    def load(k):
        at = pl.ds(k * piece, piece)
        return pltpu.make_async_copy(x_ref.at[:, at], held_ref.at[:, at], sems.at[k])

    for k in range(pieces):
        load(k).start()
    half = upright(half_ref)
    rate = upright(rate_ref)
    most = upright(graze_ref)
    prefer = prefer_ref[...]
    uptake_b = uptake_ref[...].T.astype(BF16)
    quarter = (iota((NUT, PLK), 1) // (PLK // NUT) == iota((NUT, PLK), 0)).astype(F32)
    first = jnp.concatenate([prefer, uptake_ref[...] * rate_ref[...]], axis=0).astype(BF16)
    second = jnp.concatenate(
        [
            jnp.concatenate([prefer.T, jnp.zeros((PLK, 2 * PLK), F32)], axis=1),
            jnp.concatenate([jnp.zeros((NUT, PLK), F32), quarter, quarter], axis=1),
        ],
        axis=0,
    ).astype(BF16)
    span = CHUNK // LANES

    def row_of(ref, c):
        return jnp.concatenate([ref[c * span + s : c * span + s + 1, :] for s in range(span)], axis=1)

    for c in range(cells // CHUNK):
        if c * CHUNK % piece == 0:
            load(c * CHUNK // piece).wait()
        plankton_b = plankton_sent(low_ref, high_ref, c, CHUNK)
        at = slice(c * CHUNK, (c + 1) * CHUNK)
        nutrient = held_ref[:NUT, at]
        plankton = held_ref[NUT : NUT + PLK, at]
        detritus = held_ref[NUT + PLK :, at]
        sun = row_of(light_ref, c)
        mask = row_of(wet_ref, c)
        both = dot(first, plankton_b)
        food, drawn = both[:PLK], both[PLK:]
        monod = nutrient / (nutrient + half)
        limitation = dot(uptake_b, monod.astype(BF16))
        growth = rate * sun * plankton * limitation
        graze = most * plankton / (1.0 + food)
        eaten = graze * food
        waste = (1.0 - EFFICIENCY) * eaten + MORTALITY * plankton
        waste_high = waste.astype(BF16)
        waste_low = (waste - waste_high.astype(F32)).astype(BF16)
        both = dot(second, jnp.concatenate([graze.astype(BF16), waste_high, waste_low], axis=0))
        lost, fallen = both[:PLK], both[PLK:]
        d_plankton = growth - plankton * lost + EFFICIENCY * eaten - MORTALITY * plankton
        d_nutrient = REMINERAL * detritus - monod * sun * drawn
        d_detritus = fallen - REMINERAL * detritus
        scale = TIMESTEP * mask
        base_ref[:NUT, at] = nutrient + scale * d_nutrient
        base_ref[NUT : NUT + PLK, at] = plankton + scale * d_plankton
        base_ref[NUT + PLK :, at] = detritus + scale * d_detritus
        if c % 4 == 3:
            done = pl.ds((c - 3) * CHUNK, 4 * CHUNK)
            pltpu.make_async_copy(base_ref.at[:, done], far_ref.at[:, done], sem).start()
    pltpu.make_async_copy(base_ref, far_ref, sem).wait()


def places(rows, cols, first, blocks, held):
    slot, col = rows - first, cols - first
    slot = jnp.where((slot >= 0) & (slot < blocks), slot, blocks)
    return slot, jnp.clip(jnp.where(col < 0, col + held, col), 0, held - 1)


def block_at(slot):
    return pl.ds(pl.multiple_of(slot * LANES, LANES), LANES)


def first_block(blocks):
    return (lax.axis_index("grp") * lax.axis_size("dev") + lax.axis_index("dev")) * blocks


def local_kernel(index_ref, tiles_ref, low_ref, high_ref, left_ref, right_ref, base_ref,
                 received_ref, out_ref, picked_ref, slot_ref, made_ref,
                 reach_ref, held_ref, vector_ref, far_ref, sems, base_sem, far_sem):
    cells = base_ref.shape[1]
    blocks = cells // LANES
    width = low_ref.shape[1]
    pieces = sems.shape[0]
    batch = held_ref.shape[0] // pieces
    spill = picked_ref.shape[0]
    devices = received_ref.shape[0]
    share = made_ref.shape[1] // devices

    def load(k):
        at = pl.ds(k * batch, batch)
        return pltpu.make_async_copy(tiles_ref.at[at], held_ref.at[at], sems.at[k])

    me = lax.axis_index("dev")
    row = received_ref[jnp.minimum(me + 1, devices - 1)]
    row = jnp.where(me + 1 < devices, row, -1.0).astype(jnp.int32)
    slot, col = places(row, row, first_block(blocks), blocks, 2 * blocks)
    vector_ref[...] = jnp.where(iota(row.shape, 1) < share + spill, slot, col)
    move = pltpu.make_async_copy(vector_ref, far_ref, far_sem)
    move.start()
    slot_ref[...] = pltpu.roll(slot, LANES - share, 1)
    made_ref[...] = jnp.concatenate(
        [received_ref[o][:, :share] for o in range(devices)], axis=1
    )
    part_of = lambda k: slice(k * width, (k + 1) * width)
    load(0).start()
    start = pltpu.make_async_copy(base_ref, out_ref.at[:, pl.ds(0, cells)], base_sem)
    start.start()
    for k in range(1, pieces):
        load(k).start()
    for k, ref in enumerate((low_ref, high_ref, right_ref, left_ref)):
        reach_ref[:, part_of(k)] = ref[...]
    move.wait()
    for t in range(spill):
        picked_ref[t] = reach_ref[:, block_at(far_ref[0, share + spill + t])]
    out_ref[:, cells:] = jnp.zeros((out_ref.shape[0], LANES), F32)
    start.wait()

    def piece(k, carry):
        load(k).wait()
        for j in range(batch):
            t = k * batch + j
            out_ref[:, block_at(index_ref[0, t])] += rows_dot(
                reach_ref[:, block_at(index_ref[1, t])], held_ref[t]
            )
        return carry

    lax.fori_loop(0, pieces, piece, 0)


def last_kernel(slot_ref, tiles_ref, picked_ref, mid_ref, out_ref, total_ref, out_sem):
    cells = out_ref.shape[1]
    blocks = cells // LANES

    def store(b, carry):
        at = block_at(b)
        pltpu.make_async_copy(total_ref.at[:, at], out_ref.at[:, at], out_sem).start()
        return carry

    count = tiles_ref.shape[0]
    done = 0
    for begin in (0, count // 2):
        head = slot_ref[0, begin]
        lax.fori_loop(done, head, store, 0)
        done = jnp.maximum(done, head)
        for t in range(begin, count if begin else count // 2):
            total_ref[:, block_at(slot_ref[0, t])] += rows_dot(picked_ref[t], tiles_ref[t])
    lax.fori_loop(done, blocks, store, 0)
    pltpu.make_async_copy(total_ref.at[:, pl.ds(0, cells)], out_ref, out_sem).wait()


def per_device(
    tracer, tile_rows, tile_cols, tile_values, level_counts, column_owner,
    half_saturation, growth_rate, uptake, graze_preference, graze_maximum,
):
    channels, cells = tracer.shape
    tile_total, block = tile_values.shape[0], tile_values.shape[1]
    spill = tile_total // 8
    half = cells // 2
    assert half >= REACH * block and block == LANES
    assert level_counts.shape[0] // lax.axis_size("dev") + 2 * spill <= LANES
    devices = lax.axis_size("dev")

    source = in_hbm(tracer)
    tiles = in_hbm(tile_values)
    high = rounded(source, half, half)
    low = rounded(source, 0, half)
    left = chain_shift(high, 1)
    right = chain_shift(low, -1)

    share = level_counts.shape[0] // devices
    blocks = cells // block
    send, spilled, light, wet, index = pl.pallas_call(
        produce_kernel,
        out_shape=(
            jax.ShapeDtypeStruct((devices, 1, LANES), F32),
            pltpu.HBM((spill, block, block), BF16),
            jax.ShapeDtypeStruct((blocks, LANES), F32),
            jax.ShapeDtypeStruct((blocks, LANES), F32),
            jax.ShapeDtypeStruct((2, tile_total), jnp.int32),
        ),
        in_specs=[HBM_SPEC] + [VMEM_SPEC] * 9 + [HBM_SPEC],
        out_specs=(VMEM_SPEC, HBM_SPEC) + (VMEM_SPEC,) * 3,
        scratch_shapes=[
            pltpu.VMEM((blocks, LANES), F32),
            pltpu.VMEM((blocks, LANES), F32),
            pltpu.VMEM((spill, block, block), BF16),
            pltpu.VMEM((NUT, cells), F32),
            pltpu.SemaphoreType.DMA,
            pltpu.SemaphoreType.DMA,
        ],
        compiler_params=pltpu.CompilerParams(vmem_limit_bytes=4 << 20),
        cost_estimate=pl.CostEstimate(
            flops=cells * 8000, bytes_accessed=channels * cells * 4, transcendentals=cells
        ),
    )(
        source,
        low,
        high,
        level_counts[None, :],
        column_owner[None, :],
        half_saturation[None, :],
        growth_rate[None, :],
        uptake.T,
        tile_rows[None, :],
        tile_cols[None, :],
        tiles,
    )
    received = lax.all_to_all(send, "dev", split_axis=0, concat_axis=0, tiled=True)

    more_tiles = group_shift(spilled, -1)
    base = pl.pallas_call(
        ecosystem_kernel,
        out_shape=pltpu.HBM((channels, cells), F32),
        in_specs=[HBM_SPEC] + [VMEM_SPEC] * 9,
        out_specs=HBM_SPEC,
        scratch_shapes=[pltpu.VMEM((channels, cells), F32)] * 2
        + [pltpu.SemaphoreType.DMA, pltpu.SemaphoreType.DMA((4,))],
        compiler_params=pltpu.CompilerParams(vmem_limit_bytes=4 << 20),
        cost_estimate=pl.CostEstimate(
            flops=cells * 30000, bytes_accessed=channels * cells * 8, transcendentals=0
        ),
    )(
        source,
        low,
        high,
        light,
        wet,
        half_saturation[None, :],
        growth_rate[None, :],
        uptake.T,
        graze_preference,
        graze_maximum[None, :],
    )

    smem = pl.BlockSpec(memory_space=pltpu.SMEM)
    pieces = 10
    work = 2 * channels * block * block
    mid, picked, slots, made = pl.pallas_call(
        local_kernel,
        out_shape=(
            jax.ShapeDtypeStruct((channels, cells + LANES), F32),
            jax.ShapeDtypeStruct((spill, channels, block), BF16),
            jax.ShapeDtypeStruct((1, LANES), jnp.int32),
            jax.ShapeDtypeStruct((1, devices * share), F32),
        ),
        in_specs=[smem, HBM_SPEC] + [VMEM_SPEC] * 4 + [HBM_SPEC, VMEM_SPEC],
        out_specs=(VMEM_SPEC,) * 4,
        scratch_shapes=[
            pltpu.VMEM((channels, 4 * half), BF16),
            pltpu.VMEM((tile_total, block, block), BF16),
            pltpu.VMEM((1, LANES), jnp.int32),
            pltpu.SMEM((1, LANES), jnp.int32),
            pltpu.SemaphoreType.DMA((pieces,)),
            pltpu.SemaphoreType.DMA,
            pltpu.SemaphoreType.DMA,
        ],
        compiler_params=pltpu.CompilerParams(vmem_limit_bytes=10 << 20),
        cost_estimate=pl.CostEstimate(
            flops=tile_total * work, bytes_accessed=tile_values.size * 2, transcendentals=0
        ),
    )(index, tiles, low, high, left, right, in_hbm(base), received)
    updated, _ = pl.pallas_call(
        last_kernel,
        out_shape=(
            jax.ShapeDtypeStruct((channels, cells), F32),
            jax.ShapeDtypeStruct((channels, cells + LANES), F32),
        ),
        in_specs=[smem] + [VMEM_SPEC] * 3,
        out_specs=(HBM_SPEC, VMEM_SPEC),
        scratch_shapes=[pltpu.SemaphoreType.DMA],
        input_output_aliases={3: 1},
        compiler_params=pltpu.CompilerParams(vmem_limit_bytes=6 << 20),
        cost_estimate=pl.CostEstimate(
            flops=spill * work, bytes_accessed=channels * cells * 8, transcendentals=0
        ),
    )(slots, more_tiles, picked, mid)
    return updated, made.reshape(-1)


def solution(mesh):
    return jax.shard_map(
        per_device,
        mesh=mesh,
        in_specs=(
            P(None, CHAIN),
            P(CHAIN),
            P(CHAIN),
            P(CHAIN, None, None),
            P(CHAIN),
            P(CHAIN),
            P(),
            P(),
            P(),
            P(),
            P(),
        ),
        out_specs=(P(None, CHAIN), P(CHAIN)),
        check_vma=False,
    )
```

```python
import functools

import jax
import jax.numpy as jnp
from jax import lax
from jax.experimental import pallas as pl
from jax.experimental.pallas import tpu as pltpu
from jax.sharding import PartitionSpec as P

NUT = 16
PLK = 64
LEV = 32
REACH = 16
LANES = 128
CHUNK = 256
SPAN = 512

HIGHEST = lax.Precision.HIGHEST
WATER_DECAY = 0.03
SHADE_DECAY = 0.05
EFFICIENCY = 0.3
MORTALITY = 0.1
REMINERAL = 0.2
TIMESTEP = 0.5
F32 = jnp.float32
BF16 = jnp.bfloat16
CHAIN = ("grp", "dev")


def chain_shift(x, step):
    count = lax.axis_size(CHAIN)
    pairs = [(i, i + step) for i in range(count) if 0 <= i + step < count]
    return lax.ppermute(x, CHAIN, pairs)


def down_shift(x, near):
    count, group = lax.axis_size(CHAIN), lax.axis_size("dev")
    pairs = [(i, i - 1) for i in range(1, count) if (i % group == 1) == near]
    return lax.ppermute(x, CHAIN, pairs)


def group_shift(x, step):
    count = lax.axis_size("dev")
    pairs = [(i, i + step) for i in range(count) if 0 <= i + step < count]
    return lax.ppermute(x, "dev", pairs)


def iota(shape, dim):
    return lax.broadcasted_iota(jnp.int32, shape, dim)


def rows_dot(a, b, precision=None):
    return lax.dot_general(
        a, b, (((1,), (1,)), ((), ())), precision=precision, preferred_element_type=F32
    )


def dot(a, b, precision=None):
    return jnp.dot(a, b, precision=precision, preferred_element_type=F32)


def in_hbm(x):
    return pltpu.with_memory_space_constraint(x, pltpu.HBM)


VMEM_SPEC = pl.BlockSpec(memory_space=pltpu.VMEM)
HBM_SPEC = pl.BlockSpec(memory_space=pltpu.HBM)
ANY_SPEC = pl.BlockSpec(memory_space=pl.ANY)


def round_kernel(start, x_ref, out_ref, held_ref, sems):
    pieces = sems.shape[0]
    rows, width = out_ref.shape[0] // pieces, out_ref.shape[1]

    def load(k):
        at = pl.ds(k * rows, rows)
        return pltpu.make_async_copy(
            x_ref.at[at, pl.ds(start, width)], held_ref.at[at], sems.at[k]
        )

    for k in range(pieces):
        load(k).start()
    for k in range(pieces):
        load(k).wait()
        at = slice(k * rows, (k + 1) * rows)
        out_ref[at, :] = held_ref[at, :].astype(BF16)


def rounded(x, start, width, pieces=3):
    rows = x.shape[0]
    return pl.pallas_call(
        functools.partial(round_kernel, start),
        out_shape=jax.ShapeDtypeStruct((rows, width), BF16),
        in_specs=[HBM_SPEC],
        out_specs=VMEM_SPEC,
        scratch_shapes=[pltpu.VMEM((rows, width), F32), pltpu.SemaphoreType.DMA((pieces,))],
        compiler_params=pltpu.CompilerParams(vmem_limit_bytes=4 << 20),
        cost_estimate=pl.CostEstimate(
            flops=rows * width, bytes_accessed=rows * width * 6, transcendentals=0
        ),
    )(x)


def exact_dot(a, ones):
    n = a.shape[0]
    parts, rest = [], a
    for _ in range(3):
        part = rest.astype(BF16)
        parts.append(part.astype(F32))
        rest = rest - parts[-1]
    out = dot(jnp.concatenate(parts, axis=0).astype(BF16), ones)
    return out[:n] + out[n : 2 * n] + out[2 * n :]


def upright(ref):
    n = ref.shape[1]
    return jnp.sum(
        jnp.where(iota((n, n), 0) == iota((n, n), 1), ref[...], 0.0), axis=1, keepdims=True
    )


def halves(a):
    top = a.astype(BF16)
    return top, (a - top.astype(F32)).astype(BF16)


def left_parts(a):
    top, rest = halves(a)
    return jnp.concatenate([v.astype(F32) for v in (top, rest, top)], axis=1).astype(BF16)


def right_parts(top, rest):
    return jnp.concatenate([top, top, rest], axis=0)


def plankton_sent(low_ref, high_ref, c, width):
    half = low_ref.shape[1]
    start = c * width
    ref, at = (low_ref, start) if start < half else (high_ref, start - half)
    return ref[NUT : NUT + PLK, at : at + width]


def produce_kernel(
    x_ref, low_ref, high_ref, level_ref, owner_ref, half_ref, rate_ref, uptake_ref,
    rows_ref, cols_ref, tiles_ref,
    send_ref, more_ref, light_ref, wet_ref, index_ref, sums_ref, made_ref, held_ref,
    few_ref, more_sem, few_sems,
):
    pieces = few_sems.shape[0]
    piece = x_ref.shape[1] // pieces

    def load(k):
        at = (pl.ds(0, NUT + PLK), pl.ds(k * piece, piece))
        return pltpu.make_async_copy(x_ref.at[at], few_ref.at[at], few_sems.at[k])

    for k in range(pieces):
        load(k).start()
    spill = more_ref.shape[0]
    pack = pltpu.make_async_copy(tiles_ref.at[pl.ds(0, spill)], held_ref, more_sem)
    pack.start()
    cells = x_ref.shape[1]
    blocks = cells // LANES
    slot, col = places(
        rows_ref[...], cols_ref[...], first_block(blocks), blocks, 2 * blocks
    )
    index_ref[0:1, :] = slot
    index_ref[1:2, :] = col
    per_block = LANES // LEV
    columns = level_ref.shape[1]
    devices = send_ref.shape[0]
    share = columns // devices

    half = upright(half_ref)
    weight = left_parts(
        jnp.concatenate([uptake_ref[...] * rate_ref[...], jnp.ones((NUT, PLK), F32)], axis=0)
    )
    for c in range(cells // SPAN):
        if c * SPAN % piece == 0:
            load(c * SPAN // piece).wait()
        at = slice(c * SPAN, (c + 1) * SPAN)
        top = plankton_sent(low_ref, high_ref, c, SPAN)
        rest = (few_ref[NUT:, at] - top.astype(F32)).astype(BF16)
        both = dot(weight, right_parts(top, rest))
        nutrient = few_ref[:NUT, at]
        monod = nutrient / (nutrient + half)
        total = both[NUT : NUT + 1]
        taken = jnp.sum(monod * both[:NUT], axis=0, keepdims=True)
        for s in range(SPAN // LANES):
            row = c * (SPAN // LANES) + s
            sums_ref[row : row + 1, :] = total[:, s * LANES : (s + 1) * LANES]
            made_ref[row : row + 1, :] = taken[:, s * LANES : (s + 1) * LANES]

    pack.wait()
    pack = pltpu.make_async_copy(held_ref, more_ref, more_sem)
    pack.start()

    mine = iota((blocks, columns), 1) // per_block == iota((blocks, columns), 0)
    spread = iota((columns, LANES), 0) % per_block == iota((columns, LANES), 1) // LEV
    gather = iota((LANES, columns), 1) % per_block == iota((LANES, columns), 0) // LEV
    levels = level_ref[...].astype(F32)
    counts = dot(jnp.where(mine, levels, 0.0).astype(BF16), spread.astype(BF16))
    depth = (iota((blocks, LANES), 1) % LEV).astype(F32)
    wet = (depth < counts).astype(F32)
    wet_ref[...] = wet
    upper, lower = iota((LANES, LANES), 0), iota((LANES, LANES), 1)
    above = ((upper // LEV == lower // LEV) & (upper < lower)).astype(BF16)
    shading = exact_dot(sums_ref[...] / PLK * wet, above)
    light = jnp.exp(-WATER_DECAY * depth - SHADE_DECAY * shading)
    light_ref[...] = light

    by_column = exact_dot(light * made_ref[...] / PLK * wet, gather.astype(BF16))
    production = jnp.sum(jnp.where(mine, by_column, 0.0), axis=0, keepdims=True)
    owned = owner_ref[...] == iota((devices, columns), 0)
    before = (iota((columns, columns), 0) < iota((columns, columns), 1)).astype(BF16)
    earlier = dot(owned.astype(BF16), before)
    rank = jnp.sum(jnp.where(owned, earlier, 0.0), axis=0, keepdims=True).astype(jnp.int32)
    place = (rank == iota((LANES, columns), 0)).astype(F32)
    sorted_sums = rows_dot(jnp.where(owned, production, 0.0), place, HIGHEST)
    lane = iota((1, LANES), 1)
    rows = pltpu.roll(rows_ref[:, :LANES].astype(F32), share, 1)
    cols = pltpu.roll(cols_ref[:, :LANES].astype(F32), share + spill, 1)
    index = jnp.where(lane < share + spill, rows, cols)
    for o in range(devices):
        send_ref[o] = jnp.where(lane < share, sorted_sums[o : o + 1, :], index)
    pack.wait()


def ecosystem_kernel(
    x_ref, low_ref, high_ref, light_ref, wet_ref, half_ref, rate_ref, uptake_ref, prefer_ref,
    graze_ref,
    far_ref, base_ref, held_ref, sem, sems,
):
    cells = x_ref.shape[1]
    pieces = sems.shape[0]
    piece = cells // pieces

    def load(k):
        at = pl.ds(k * piece, piece)
        return pltpu.make_async_copy(x_ref.at[:, at], held_ref.at[:, at], sems.at[k])

    for k in range(pieces):
        load(k).start()
    half = upright(half_ref)
    rate = upright(rate_ref)
    most = upright(graze_ref)
    prefer = prefer_ref[...]
    uptake_b = left_parts(uptake_ref[...].T)
    quarter = (iota((NUT, PLK), 1) // (PLK // NUT) == iota((NUT, PLK), 0)).astype(F32)
    quarter_b = jnp.concatenate([quarter, quarter], axis=1).astype(BF16)
    first = left_parts(jnp.concatenate([prefer, uptake_ref[...] * rate_ref[...]], axis=0))
    second = left_parts(prefer.T)
    span = CHUNK // LANES

    def row_of(ref, c):
        return jnp.concatenate([ref[c * span + s : c * span + s + 1, :] for s in range(span)], axis=1)

    for c in range(cells // CHUNK):
        if c * CHUNK % piece == 0:
            load(c * CHUNK // piece).wait()
        plankton_b = plankton_sent(low_ref, high_ref, c, CHUNK)
        at = slice(c * CHUNK, (c + 1) * CHUNK)
        nutrient = held_ref[:NUT, at]
        plankton = held_ref[NUT : NUT + PLK, at]
        detritus = held_ref[NUT + PLK :, at]
        sun = row_of(light_ref, c)
        mask = row_of(wet_ref, c)
        rest = (plankton - plankton_b.astype(F32)).astype(BF16)
        both = dot(first, right_parts(plankton_b, rest))
        food, drawn = both[:PLK], both[PLK:]
        monod = nutrient / (nutrient + half)
        limitation = dot(uptake_b, right_parts(*halves(monod)))
        growth = rate * sun * plankton * limitation
        graze = most * plankton / (1.0 + food)
        eaten = graze * food
        waste = (1.0 - EFFICIENCY) * eaten + MORTALITY * plankton
        lost = dot(second, right_parts(*halves(graze)))
        fallen = dot(quarter_b, jnp.concatenate(halves(waste), axis=0))
        d_plankton = growth - plankton * lost + EFFICIENCY * eaten - MORTALITY * plankton
        d_nutrient = REMINERAL * detritus - monod * sun * drawn
        d_detritus = fallen - REMINERAL * detritus
        scale = TIMESTEP * mask
        base_ref[:NUT, at] = nutrient + scale * d_nutrient
        base_ref[NUT : NUT + PLK, at] = plankton + scale * d_plankton
        base_ref[NUT + PLK :, at] = detritus + scale * d_detritus
        if c % 4 == 3:
            done = pl.ds((c - 3) * CHUNK, 4 * CHUNK)
            pltpu.make_async_copy(base_ref.at[:, done], far_ref.at[:, done], sem).start()
    pltpu.make_async_copy(base_ref, far_ref, sem).wait()


def places(rows, cols, first, blocks, held):
    slot, col = rows - first, cols - first
    slot = jnp.where((slot >= 0) & (slot < blocks), slot, blocks)
    return slot, jnp.clip(jnp.where(col < 0, col + held, col), 0, held - 1)


def block_at(slot):
    return pl.ds(pl.multiple_of(slot * LANES, LANES), LANES)


def first_block(blocks):
    return (lax.axis_index("grp") * lax.axis_size("dev") + lax.axis_index("dev")) * blocks


def local_kernel(index_ref, tiles_ref, low_ref, high_ref, left_ref, right_ref, near_ref, base_ref,
                 received_ref, out_ref, picked_ref, slot_ref, made_ref,
                 reach_ref, held_ref, vector_ref, far_ref, sems, base_sem, far_sem):
    cells = base_ref.shape[1]
    blocks = cells // LANES
    width = low_ref.shape[1]
    pieces = sems.shape[0]
    batch = held_ref.shape[0] // pieces
    spill = picked_ref.shape[0]
    devices = received_ref.shape[0]
    share = made_ref.shape[1] // devices

    def load(k):
        at = pl.ds(k * batch, batch)
        return pltpu.make_async_copy(tiles_ref.at[at], held_ref.at[at], sems.at[k])

    me = lax.axis_index("dev")
    row = received_ref[jnp.minimum(me + 1, devices - 1)]
    row = jnp.where(me + 1 < devices, row, -1.0).astype(jnp.int32)
    slot, col = places(row, row, first_block(blocks), blocks, 2 * blocks)
    vector_ref[...] = jnp.where(iota(row.shape, 1) < share + spill, slot, col)
    move = pltpu.make_async_copy(vector_ref, far_ref, far_sem)
    move.start()
    slot_ref[...] = pltpu.roll(slot, LANES - share, 1)
    made_ref[...] = jnp.concatenate(
        [received_ref[o][:, :share] for o in range(devices)], axis=1
    )
    part_of = lambda k: slice(k * width, (k + 1) * width)
    load(0).start()
    start = pltpu.make_async_copy(base_ref, out_ref.at[:, pl.ds(0, cells)], base_sem)
    start.start()
    for k in range(1, pieces):
        load(k).start()
    for k, ref in enumerate((low_ref, high_ref, right_ref, left_ref)):
        reach_ref[:, part_of(k)] = ref[...] + near_ref[...] if k == 2 else ref[...]
    move.wait()
    for t in range(spill):
        picked_ref[t] = reach_ref[:, block_at(far_ref[0, share + spill + t])]
    out_ref[:, cells:] = jnp.zeros((out_ref.shape[0], LANES), F32)
    start.wait()

    def piece(k, carry):
        load(k).wait()
        for j in range(batch):
            t = k * batch + j
            out_ref[:, block_at(index_ref[0, t])] += rows_dot(
                reach_ref[:, block_at(index_ref[1, t])], held_ref[t]
            )
        return carry

    lax.fori_loop(0, pieces, piece, 0)


def last_kernel(slot_ref, tiles_ref, picked_ref, mid_ref, out_ref, total_ref, out_sem):
    cells = out_ref.shape[1]
    blocks = cells // LANES

    def store(b, carry):
        at = block_at(b)
        pltpu.make_async_copy(total_ref.at[:, at], out_ref.at[:, at], out_sem).start()
        return carry

    count = tiles_ref.shape[0]
    done = 0
    step = pl.cdiv(count, 4)
    for begin in range(0, count, step):
        head = slot_ref[0, begin]
        lax.fori_loop(done, head, store, 0)
        done = jnp.maximum(done, head)
        for t in range(begin, min(begin + step, count)):
            total_ref[:, block_at(slot_ref[0, t])] += rows_dot(picked_ref[t], tiles_ref[t])
    lax.fori_loop(done, blocks, store, 0)
    pltpu.make_async_copy(total_ref.at[:, pl.ds(0, cells)], out_ref, out_sem).wait()


def per_device(
    tracer, tile_rows, tile_cols, tile_values, level_counts, column_owner,
    half_saturation, growth_rate, uptake, graze_preference, graze_maximum,
):
    channels, cells = tracer.shape
    tile_total, block = tile_values.shape[0], tile_values.shape[1]
    spill = tile_total // 8
    half = cells // 2
    assert half >= REACH * block and block == LANES
    assert level_counts.shape[0] // lax.axis_size("dev") + 2 * spill <= LANES
    devices = lax.axis_size("dev")

    source = in_hbm(tracer)
    tiles = in_hbm(tile_values)
    high = rounded(source, half, half)
    low = rounded(source, 0, half)
    left = chain_shift(high, 1)
    right = down_shift(low, False)
    near = down_shift(low, True)

    share = level_counts.shape[0] // devices
    blocks = cells // block
    send, spilled, light, wet, index = pl.pallas_call(
        produce_kernel,
        out_shape=(
            jax.ShapeDtypeStruct((devices, 1, LANES), F32),
            pltpu.HBM((spill, block, block), BF16),
            jax.ShapeDtypeStruct((blocks, LANES), F32),
            jax.ShapeDtypeStruct((blocks, LANES), F32),
            jax.ShapeDtypeStruct((2, tile_total), jnp.int32),
        ),
        in_specs=[HBM_SPEC] + [VMEM_SPEC] * 9 + [HBM_SPEC],
        out_specs=(VMEM_SPEC, HBM_SPEC) + (VMEM_SPEC,) * 3,
        scratch_shapes=[
            pltpu.VMEM((blocks, LANES), F32),
            pltpu.VMEM((blocks, LANES), F32),
            pltpu.VMEM((spill, block, block), BF16),
            pltpu.VMEM((NUT + PLK, cells), F32),
            pltpu.SemaphoreType.DMA,
            pltpu.SemaphoreType.DMA((4,)),
        ],
        compiler_params=pltpu.CompilerParams(vmem_limit_bytes=4 << 20),
        cost_estimate=pl.CostEstimate(
            flops=cells * 8000, bytes_accessed=channels * cells * 4, transcendentals=cells
        ),
    )(
        source,
        low,
        high,
        level_counts[None, :],
        column_owner[None, :],
        half_saturation[None, :],
        growth_rate[None, :],
        uptake.T,
        tile_rows[None, :],
        tile_cols[None, :],
        tiles,
    )
    received = lax.all_to_all(send, "dev", split_axis=0, concat_axis=0, tiled=True)

    more_tiles = group_shift(spilled, -1)
    base = pl.pallas_call(
        ecosystem_kernel,
        out_shape=pltpu.HBM((channels, cells), F32),
        in_specs=[HBM_SPEC] + [VMEM_SPEC] * 9,
        out_specs=HBM_SPEC,
        scratch_shapes=[pltpu.VMEM((channels, cells), F32)] * 2
        + [pltpu.SemaphoreType.DMA, pltpu.SemaphoreType.DMA((4,))],
        compiler_params=pltpu.CompilerParams(vmem_limit_bytes=4 << 20),
        cost_estimate=pl.CostEstimate(
            flops=cells * 30000, bytes_accessed=channels * cells * 8, transcendentals=0
        ),
    )(
        source,
        low,
        high,
        light,
        wet,
        half_saturation[None, :],
        growth_rate[None, :],
        uptake.T,
        graze_preference,
        graze_maximum[None, :],
    )

    smem = pl.BlockSpec(memory_space=pltpu.SMEM)
    pieces = 10
    work = 2 * channels * block * block
    mid, picked, slots, made = pl.pallas_call(
        local_kernel,
        out_shape=(
            jax.ShapeDtypeStruct((channels, cells + LANES), F32),
            jax.ShapeDtypeStruct((spill, channels, block), BF16),
            jax.ShapeDtypeStruct((1, LANES), jnp.int32),
            jax.ShapeDtypeStruct((1, devices * share), F32),
        ),
        in_specs=[smem, HBM_SPEC] + [VMEM_SPEC] * 5 + [HBM_SPEC, VMEM_SPEC],
        out_specs=(VMEM_SPEC,) * 4,
        scratch_shapes=[
            pltpu.VMEM((channels, 4 * half), BF16),
            pltpu.VMEM((tile_total, block, block), BF16),
            pltpu.VMEM((1, LANES), jnp.int32),
            pltpu.SMEM((1, LANES), jnp.int32),
            pltpu.SemaphoreType.DMA((pieces,)),
            pltpu.SemaphoreType.DMA,
            pltpu.SemaphoreType.DMA,
        ],
        compiler_params=pltpu.CompilerParams(vmem_limit_bytes=10 << 20),
        cost_estimate=pl.CostEstimate(
            flops=tile_total * work, bytes_accessed=tile_values.size * 2, transcendentals=0
        ),
    )(index, tiles, low, high, left, right, near, in_hbm(base), received)
    updated, _ = pl.pallas_call(
        last_kernel,
        out_shape=(
            jax.ShapeDtypeStruct((channels, cells), F32),
            jax.ShapeDtypeStruct((channels, cells + LANES), F32),
        ),
        in_specs=[smem] + [VMEM_SPEC] * 3,
        out_specs=(HBM_SPEC, VMEM_SPEC),
        scratch_shapes=[pltpu.SemaphoreType.DMA],
        input_output_aliases={3: 1},
        compiler_params=pltpu.CompilerParams(vmem_limit_bytes=6 << 20),
        cost_estimate=pl.CostEstimate(
            flops=spill * work, bytes_accessed=channels * cells * 8, transcendentals=0
        ),
    )(slots, more_tiles, picked, mid)
    return updated, made.reshape(-1)


def solution(mesh):
    return jax.shard_map(
        per_device,
        mesh=mesh,
        in_specs=(
            P(None, CHAIN),
            P(CHAIN),
            P(CHAIN),
            P(CHAIN, None, None),
            P(CHAIN),
            P(CHAIN),
            P(),
            P(),
            P(),
            P(),
            P(),
        ),
        out_specs=(P(None, CHAIN), P(CHAIN)),
        check_vma=False,
    )
```

```python
import functools

import jax
import jax.numpy as jnp
from jax import lax
from jax.experimental import pallas as pl
from jax.experimental.pallas import tpu as pltpu
from jax.sharding import PartitionSpec as P

NUT = 16
PLK = 64
LEV = 32
REACH = 16
LANES = 128
CHUNK = 256
SPAN = 512

HIGHEST = lax.Precision.HIGHEST
WATER_DECAY = 0.03
SHADE_DECAY = 0.05
EFFICIENCY = 0.3
MORTALITY = 0.1
REMINERAL = 0.2
TIMESTEP = 0.5
F32 = jnp.float32
BF16 = jnp.bfloat16
CHAIN = ("grp", "dev")


def chain_shift(x, step):
    count = lax.axis_size(CHAIN)
    pairs = [(i, i + step) for i in range(count) if 0 <= i + step < count]
    return lax.ppermute(x, CHAIN, pairs)


def down_shift(x, near):
    count, group = lax.axis_size(CHAIN), lax.axis_size("dev")
    pairs = [(i, i - 1) for i in range(1, count) if (i % group <= 1) == near]
    return lax.ppermute(x, CHAIN, pairs)


def group_shift(x, step):
    count = lax.axis_size("dev")
    pairs = [(i, i + step) for i in range(count) if 0 <= i + step < count]
    return lax.ppermute(x, "dev", pairs)


def iota(shape, dim):
    return lax.broadcasted_iota(jnp.int32, shape, dim)


def rows_dot(a, b, precision=None):
    return lax.dot_general(
        a, b, (((1,), (1,)), ((), ())), precision=precision, preferred_element_type=F32
    )


def dot(a, b, precision=None):
    return jnp.dot(a, b, precision=precision, preferred_element_type=F32)


def in_hbm(x):
    return pltpu.with_memory_space_constraint(x, pltpu.HBM)


VMEM_SPEC = pl.BlockSpec(memory_space=pltpu.VMEM)
HBM_SPEC = pl.BlockSpec(memory_space=pltpu.HBM)
ANY_SPEC = pl.BlockSpec(memory_space=pl.ANY)


def round_kernel(start, x_ref, out_ref, held_ref, sems):
    pieces = sems.shape[0]
    rows, width = out_ref.shape[0] // pieces, out_ref.shape[1]

    def load(k):
        at = pl.ds(k * rows, rows)
        return pltpu.make_async_copy(
            x_ref.at[at, pl.ds(start, width)], held_ref.at[at], sems.at[k]
        )

    for k in range(pieces):
        load(k).start()
    for k in range(pieces):
        load(k).wait()
        at = slice(k * rows, (k + 1) * rows)
        out_ref[at, :] = held_ref[at, :].astype(BF16)


def rounded(x, start, width, pieces=3):
    rows = x.shape[0]
    return pl.pallas_call(
        functools.partial(round_kernel, start),
        out_shape=jax.ShapeDtypeStruct((rows, width), BF16),
        in_specs=[HBM_SPEC],
        out_specs=VMEM_SPEC,
        scratch_shapes=[pltpu.VMEM((rows, width), F32), pltpu.SemaphoreType.DMA((pieces,))],
        compiler_params=pltpu.CompilerParams(vmem_limit_bytes=4 << 20),
        cost_estimate=pl.CostEstimate(
            flops=rows * width, bytes_accessed=rows * width * 6, transcendentals=0
        ),
    )(x)


def exact_dot(a, ones):
    n = a.shape[0]
    parts, rest = [], a
    for _ in range(3):
        part = rest.astype(BF16)
        parts.append(part.astype(F32))
        rest = rest - parts[-1]
    out = dot(jnp.concatenate(parts, axis=0).astype(BF16), ones)
    return out[:n] + out[n : 2 * n] + out[2 * n :]


def upright(ref):
    n = ref.shape[1]
    return jnp.sum(
        jnp.where(iota((n, n), 0) == iota((n, n), 1), ref[...], 0.0), axis=1, keepdims=True
    )


def halves(a):
    top = a.astype(BF16)
    return top, (a - top.astype(F32)).astype(BF16)


def left_parts(a):
    top, rest = halves(a)
    return jnp.concatenate([v.astype(F32) for v in (top, rest, top)], axis=1).astype(BF16)


def right_parts(top, rest):
    return jnp.concatenate([top, top, rest], axis=0)


def plankton_sent(low_ref, high_ref, c, width):
    half = low_ref.shape[1]
    start = c * width
    ref, at = (low_ref, start) if start < half else (high_ref, start - half)
    return ref[NUT : NUT + PLK, at : at + width]


def produce_kernel(
    x_ref, low_ref, high_ref, level_ref, owner_ref, half_ref, rate_ref, uptake_ref,
    rows_ref, cols_ref, tiles_ref,
    send_ref, more_ref, light_ref, wet_ref, index_ref, sums_ref, made_ref, held_ref,
    few_ref, more_sem, few_sems,
):
    pieces = few_sems.shape[0]
    piece = x_ref.shape[1] // pieces

    def load(k):
        at = (pl.ds(0, NUT + PLK), pl.ds(k * piece, piece))
        return pltpu.make_async_copy(x_ref.at[at], few_ref.at[at], few_sems.at[k])

    for k in range(pieces):
        load(k).start()
    spill = more_ref.shape[0]
    pack = pltpu.make_async_copy(tiles_ref.at[pl.ds(0, spill)], held_ref, more_sem)
    pack.start()
    cells = x_ref.shape[1]
    blocks = cells // LANES
    slot, col = places(
        rows_ref[...], cols_ref[...], first_block(blocks), blocks, 2 * blocks
    )
    index_ref[0:1, :] = slot
    index_ref[1:2, :] = col
    per_block = LANES // LEV
    columns = level_ref.shape[1]
    devices = send_ref.shape[0]
    share = columns // devices

    half = upright(half_ref)
    weight = left_parts(
        jnp.concatenate([uptake_ref[...] * rate_ref[...], jnp.ones((NUT, PLK), F32)], axis=0)
    )
    for c in range(cells // SPAN):
        if c * SPAN % piece == 0:
            load(c * SPAN // piece).wait()
        at = slice(c * SPAN, (c + 1) * SPAN)
        top = plankton_sent(low_ref, high_ref, c, SPAN)
        rest = (few_ref[NUT:, at] - top.astype(F32)).astype(BF16)
        both = dot(weight, right_parts(top, rest))
        nutrient = few_ref[:NUT, at]
        monod = nutrient / (nutrient + half)
        total = both[NUT : NUT + 1]
        taken = jnp.sum(monod * both[:NUT], axis=0, keepdims=True)
        for s in range(SPAN // LANES):
            row = c * (SPAN // LANES) + s
            sums_ref[row : row + 1, :] = total[:, s * LANES : (s + 1) * LANES]
            made_ref[row : row + 1, :] = taken[:, s * LANES : (s + 1) * LANES]

    pack.wait()
    pack = pltpu.make_async_copy(held_ref, more_ref, more_sem)
    pack.start()

    mine = iota((blocks, columns), 1) // per_block == iota((blocks, columns), 0)
    spread = iota((columns, LANES), 0) % per_block == iota((columns, LANES), 1) // LEV
    gather = iota((LANES, columns), 1) % per_block == iota((LANES, columns), 0) // LEV
    levels = level_ref[...].astype(F32)
    counts = dot(jnp.where(mine, levels, 0.0).astype(BF16), spread.astype(BF16))
    depth = (iota((blocks, LANES), 1) % LEV).astype(F32)
    wet = (depth < counts).astype(F32)
    wet_ref[...] = wet
    upper, lower = iota((LANES, LANES), 0), iota((LANES, LANES), 1)
    above = ((upper // LEV == lower // LEV) & (upper < lower)).astype(BF16)
    shading = exact_dot(sums_ref[...] / PLK * wet, above)
    light = jnp.exp(-WATER_DECAY * depth - SHADE_DECAY * shading)
    light_ref[...] = light

    by_column = exact_dot(light * made_ref[...] / PLK * wet, gather.astype(BF16))
    production = jnp.sum(jnp.where(mine, by_column, 0.0), axis=0, keepdims=True)
    owned = owner_ref[...] == iota((devices, columns), 0)
    before = (iota((columns, columns), 0) < iota((columns, columns), 1)).astype(BF16)
    earlier = dot(owned.astype(BF16), before)
    rank = jnp.sum(jnp.where(owned, earlier, 0.0), axis=0, keepdims=True).astype(jnp.int32)
    place = (rank == iota((LANES, columns), 0)).astype(F32)
    sorted_sums = rows_dot(jnp.where(owned, production, 0.0), place, HIGHEST)
    lane = iota((1, LANES), 1)
    rows = pltpu.roll(rows_ref[:, :LANES].astype(F32), share, 1)
    cols = pltpu.roll(cols_ref[:, :LANES].astype(F32), share + spill, 1)
    index = jnp.where(lane < share + spill, rows, cols)
    for o in range(devices):
        send_ref[o] = jnp.where(lane < share, sorted_sums[o : o + 1, :], index)
    pack.wait()


def ecosystem_kernel(
    x_ref, low_ref, high_ref, light_ref, wet_ref, half_ref, rate_ref, uptake_ref, prefer_ref,
    graze_ref,
    far_ref, base_ref, held_ref, sem, sems,
):
    cells = x_ref.shape[1]
    pieces = sems.shape[0]
    piece = cells // pieces

    def load(k):
        at = pl.ds(k * piece, piece)
        return pltpu.make_async_copy(x_ref.at[:, at], held_ref.at[:, at], sems.at[k])

    for k in range(pieces):
        load(k).start()
    half = upright(half_ref)
    rate = upright(rate_ref)
    most = upright(graze_ref)
    prefer = prefer_ref[...]
    uptake_b = left_parts(uptake_ref[...].T)
    quarter = (iota((NUT, PLK), 1) // (PLK // NUT) == iota((NUT, PLK), 0)).astype(F32)
    quarter_b = jnp.concatenate([quarter, quarter], axis=1).astype(BF16)
    first = left_parts(jnp.concatenate([prefer, uptake_ref[...] * rate_ref[...]], axis=0))
    second = left_parts(prefer.T)
    span = CHUNK // LANES

    def row_of(ref, c):
        return jnp.concatenate([ref[c * span + s : c * span + s + 1, :] for s in range(span)], axis=1)

    for c in range(cells // CHUNK):
        if c * CHUNK % piece == 0:
            load(c * CHUNK // piece).wait()
        plankton_b = plankton_sent(low_ref, high_ref, c, CHUNK)
        at = slice(c * CHUNK, (c + 1) * CHUNK)
        nutrient = held_ref[:NUT, at]
        plankton = held_ref[NUT : NUT + PLK, at]
        detritus = held_ref[NUT + PLK :, at]
        sun = row_of(light_ref, c)
        mask = row_of(wet_ref, c)
        rest = (plankton - plankton_b.astype(F32)).astype(BF16)
        both = dot(first, right_parts(plankton_b, rest))
        food, drawn = both[:PLK], both[PLK:]
        monod = nutrient / (nutrient + half)
        limitation = dot(uptake_b, right_parts(*halves(monod)))
        growth = rate * sun * plankton * limitation
        graze = most * plankton / (1.0 + food)
        eaten = graze * food
        waste = (1.0 - EFFICIENCY) * eaten + MORTALITY * plankton
        lost = dot(second, right_parts(*halves(graze)))
        fallen = dot(quarter_b, jnp.concatenate(halves(waste), axis=0))
        d_plankton = growth - plankton * lost + EFFICIENCY * eaten - MORTALITY * plankton
        d_nutrient = REMINERAL * detritus - monod * sun * drawn
        d_detritus = fallen - REMINERAL * detritus
        scale = TIMESTEP * mask
        base_ref[:NUT, at] = nutrient + scale * d_nutrient
        base_ref[NUT : NUT + PLK, at] = plankton + scale * d_plankton
        base_ref[NUT + PLK :, at] = detritus + scale * d_detritus
        if c % 4 == 3:
            done = pl.ds((c - 3) * CHUNK, 4 * CHUNK)
            pltpu.make_async_copy(base_ref.at[:, done], far_ref.at[:, done], sem).start()
    pltpu.make_async_copy(base_ref, far_ref, sem).wait()


def places(rows, cols, first, blocks, held):
    slot, col = rows - first, cols - first
    slot = jnp.where((slot >= 0) & (slot < blocks), slot, blocks)
    return slot, jnp.clip(jnp.where(col < 0, col + held, col), 0, held - 1)


def block_at(slot):
    return pl.ds(pl.multiple_of(slot * LANES, LANES), LANES)


def first_block(blocks):
    return (lax.axis_index("grp") * lax.axis_size("dev") + lax.axis_index("dev")) * blocks


def local_kernel(index_ref, tiles_ref, low_ref, high_ref, left_ref, right_ref, near_ref, base_ref,
                 received_ref, out_ref, picked_ref, slot_ref, made_ref,
                 reach_ref, held_ref, vector_ref, far_ref, sems, base_sem, far_sem):
    cells = base_ref.shape[1]
    blocks = cells // LANES
    width = low_ref.shape[1]
    pieces = sems.shape[0]
    batch = held_ref.shape[0] // pieces
    spill = picked_ref.shape[0]
    devices = received_ref.shape[0]
    share = made_ref.shape[1] // devices

    def load(k):
        at = pl.ds(k * batch, batch)
        return pltpu.make_async_copy(tiles_ref.at[at], held_ref.at[at], sems.at[k])

    me = lax.axis_index("dev")
    row = received_ref[jnp.minimum(me + 1, devices - 1)]
    row = jnp.where(me + 1 < devices, row, -1.0).astype(jnp.int32)
    slot, col = places(row, row, first_block(blocks), blocks, 2 * blocks)
    vector_ref[...] = jnp.where(iota(row.shape, 1) < share + spill, slot, col)
    move = pltpu.make_async_copy(vector_ref, far_ref, far_sem)
    move.start()
    slot_ref[...] = pltpu.roll(slot, LANES - share, 1)
    made_ref[...] = jnp.concatenate(
        [received_ref[o][:, :share] for o in range(devices)], axis=1
    )
    part_of = lambda k: slice(k * width, (k + 1) * width)
    load(0).start()
    start = pltpu.make_async_copy(base_ref, out_ref.at[:, pl.ds(0, cells)], base_sem)
    start.start()
    for k in range(1, pieces):
        load(k).start()
    for k, ref in enumerate((low_ref, high_ref, right_ref, left_ref)):
        reach_ref[:, part_of(k)] = ref[...] + near_ref[...] if k == 2 else ref[...]
    move.wait()
    for t in range(spill):
        picked_ref[t] = reach_ref[:, block_at(far_ref[0, share + spill + t])]
    out_ref[:, cells:] = jnp.zeros((out_ref.shape[0], LANES), F32)
    start.wait()

    def piece(k, carry):
        load(k).wait()
        for j in range(batch):
            t = k * batch + j
            out_ref[:, block_at(index_ref[0, t])] += rows_dot(
                reach_ref[:, block_at(index_ref[1, t])], held_ref[t]
            )
        return carry

    lax.fori_loop(0, pieces, piece, 0)


def last_kernel(slot_ref, tiles_ref, picked_ref, mid_ref, out_ref, total_ref, out_sem):
    cells = out_ref.shape[1]
    blocks = cells // LANES

    def store(b, carry):
        at = block_at(b)
        pltpu.make_async_copy(total_ref.at[:, at], out_ref.at[:, at], out_sem).start()
        return carry

    count = tiles_ref.shape[0]
    done = 0
    for begin in (0, count // 2):
        head = slot_ref[0, begin]
        lax.fori_loop(done, head, store, 0)
        done = jnp.maximum(done, head)
        for t in range(begin, count if begin else count // 2):
            total_ref[:, block_at(slot_ref[0, t])] += rows_dot(picked_ref[t], tiles_ref[t])
    lax.fori_loop(done, blocks, store, 0)
    pltpu.make_async_copy(total_ref.at[:, pl.ds(0, cells)], out_ref, out_sem).wait()


def per_device(
    tracer, tile_rows, tile_cols, tile_values, level_counts, column_owner,
    half_saturation, growth_rate, uptake, graze_preference, graze_maximum,
):
    channels, cells = tracer.shape
    tile_total, block = tile_values.shape[0], tile_values.shape[1]
    spill = tile_total // 8
    half = cells // 2
    assert half >= REACH * block and block == LANES
    assert level_counts.shape[0] // lax.axis_size("dev") + 2 * spill <= LANES
    devices = lax.axis_size("dev")

    source = in_hbm(tracer)
    tiles = in_hbm(tile_values)
    high = rounded(source, half, half)
    low = rounded(source, 0, half)
    left = chain_shift(high, 1)
    right = down_shift(low, False)
    near = down_shift(low, True)

    share = level_counts.shape[0] // devices
    blocks = cells // block
    send, spilled, light, wet, index = pl.pallas_call(
        produce_kernel,
        out_shape=(
            jax.ShapeDtypeStruct((devices, 1, LANES), F32),
            pltpu.HBM((spill, block, block), BF16),
            jax.ShapeDtypeStruct((blocks, LANES), F32),
            jax.ShapeDtypeStruct((blocks, LANES), F32),
            jax.ShapeDtypeStruct((2, tile_total), jnp.int32),
        ),
        in_specs=[HBM_SPEC] + [VMEM_SPEC] * 9 + [HBM_SPEC],
        out_specs=(VMEM_SPEC, HBM_SPEC) + (VMEM_SPEC,) * 3,
        scratch_shapes=[
            pltpu.VMEM((blocks, LANES), F32),
            pltpu.VMEM((blocks, LANES), F32),
            pltpu.VMEM((spill, block, block), BF16),
            pltpu.VMEM((NUT + PLK, cells), F32),
            pltpu.SemaphoreType.DMA,
            pltpu.SemaphoreType.DMA((4,)),
        ],
        compiler_params=pltpu.CompilerParams(vmem_limit_bytes=4 << 20),
        cost_estimate=pl.CostEstimate(
            flops=cells * 8000, bytes_accessed=channels * cells * 4, transcendentals=cells
        ),
    )(
        source,
        low,
        high,
        level_counts[None, :],
        column_owner[None, :],
        half_saturation[None, :],
        growth_rate[None, :],
        uptake.T,
        tile_rows[None, :],
        tile_cols[None, :],
        tiles,
    )
    received = lax.all_to_all(send, "dev", split_axis=0, concat_axis=0, tiled=True)

    more_tiles = group_shift(spilled, -1)
    base = pl.pallas_call(
        ecosystem_kernel,
        out_shape=pltpu.HBM((channels, cells), F32),
        in_specs=[HBM_SPEC] + [VMEM_SPEC] * 9,
        out_specs=HBM_SPEC,
        scratch_shapes=[pltpu.VMEM((channels, cells), F32)] * 2
        + [pltpu.SemaphoreType.DMA, pltpu.SemaphoreType.DMA((4,))],
        compiler_params=pltpu.CompilerParams(vmem_limit_bytes=4 << 20),
        cost_estimate=pl.CostEstimate(
            flops=cells * 30000, bytes_accessed=channels * cells * 8, transcendentals=0
        ),
    )(
        source,
        low,
        high,
        light,
        wet,
        half_saturation[None, :],
        growth_rate[None, :],
        uptake.T,
        graze_preference,
        graze_maximum[None, :],
    )

    smem = pl.BlockSpec(memory_space=pltpu.SMEM)
    pieces = 10
    work = 2 * channels * block * block
    mid, picked, slots, made = pl.pallas_call(
        local_kernel,
        out_shape=(
            jax.ShapeDtypeStruct((channels, cells + LANES), F32),
            jax.ShapeDtypeStruct((spill, channels, block), BF16),
            jax.ShapeDtypeStruct((1, LANES), jnp.int32),
            jax.ShapeDtypeStruct((1, devices * share), F32),
        ),
        in_specs=[smem, HBM_SPEC] + [VMEM_SPEC] * 5 + [HBM_SPEC, VMEM_SPEC],
        out_specs=(VMEM_SPEC,) * 4,
        scratch_shapes=[
            pltpu.VMEM((channels, 4 * half), BF16),
            pltpu.VMEM((tile_total, block, block), BF16),
            pltpu.VMEM((1, LANES), jnp.int32),
            pltpu.SMEM((1, LANES), jnp.int32),
            pltpu.SemaphoreType.DMA((pieces,)),
            pltpu.SemaphoreType.DMA,
            pltpu.SemaphoreType.DMA,
        ],
        compiler_params=pltpu.CompilerParams(vmem_limit_bytes=10 << 20),
        cost_estimate=pl.CostEstimate(
            flops=tile_total * work, bytes_accessed=tile_values.size * 2, transcendentals=0
        ),
    )(index, tiles, low, high, left, right, near, in_hbm(base), received)
    updated, _ = pl.pallas_call(
        last_kernel,
        out_shape=(
            jax.ShapeDtypeStruct((channels, cells), F32),
            jax.ShapeDtypeStruct((channels, cells + LANES), F32),
        ),
        in_specs=[smem] + [VMEM_SPEC] * 3,
        out_specs=(HBM_SPEC, VMEM_SPEC),
        scratch_shapes=[pltpu.SemaphoreType.DMA],
        input_output_aliases={3: 1},
        compiler_params=pltpu.CompilerParams(vmem_limit_bytes=6 << 20),
        cost_estimate=pl.CostEstimate(
            flops=spill * work, bytes_accessed=channels * cells * 8, transcendentals=0
        ),
    )(slots, more_tiles, picked, mid)
    return updated, made.reshape(-1)


def solution(mesh):
    return jax.shard_map(
        per_device,
        mesh=mesh,
        in_specs=(
            P(None, CHAIN),
            P(CHAIN),
            P(CHAIN),
            P(CHAIN, None, None),
            P(CHAIN),
            P(CHAIN),
            P(),
            P(),
            P(),
            P(),
            P(),
        ),
        out_specs=(P(None, CHAIN), P(CHAIN)),
        check_vma=False,
    )
```
